128 devices in a mesh: seg: 2 (over core), dp: 64 (over z, y, x).
Axes of the slice: x: 4, y: 4, z: 4, core: 2. Of those that a mesh axis runs over, the one named last changes fastest.
Arguments:
- query_rows: bfloat16 [64, 1024, 1280], P('dp', 'seg'), may hold values from -160 to 160
- key_rows: bfloat16 [64, 1024, 1280], P('dp', 'seg'), may hold values from -8 to 8
- value_rows: bfloat16 [64, 1024, 1280], P('dp', 'seg'), may hold values from -6 to 6
- prompt_keys: bfloat16 [64, 100, 1280], P('dp', 'seg'), may hold values from -6 to 6
- prompt_values: bfloat16 [64, 100, 1280], P('dp', 'seg'), may hold values from -6 to 6
- out_grad: bfloat16 [64, 1024, 2560], P('dp', 'seg'), may hold values from -54 to 54
- w_out: bfloat16 [1280, 2560], replicated, may hold values from -0.15625 to 0.15625
Outputs:
- query_grad: bfloat16 [64, 1024, 1280], P('dp', 'seg')
- key_grad: bfloat16 [64, 1024, 1280], P('dp', 'seg')
- value_grad: bfloat16 [64, 1024, 1280], P('dp', 'seg')
- prompt_key_grad: bfloat16 [64, 100, 1280], P('dp', 'seg')
- prompt_value_grad: bfloat16 [64, 100, 1280], P('dp', 'seg')
- weight_grad: bfloat16 [1280, 2560], replicated
The draws below stay inside these ranges and needn't reach their ends.
All inputs are finite; a program needn't handle non-finite values.
Results may differ from the reference program's by a relative error of at most 0.0058.
Values may be sent and summed in bfloat16 or wider, within the bound.
No kernel may reach another device: no remote copies, remote signals or barrier semaphores. Data moves between devices by JAX's collectives and lax.ppermute only.
A program may use at most 256 MiB of HBM per device.

```python
import jax
import jax.numpy as jnp
from jax import lax

D = 2560
HEADS = 16
HD = 80
SUMS = 50
TOK = 512
SEQ = 1024
DOCS = 64
N_SEG = 2


def pair_rows(key):
    shape = (DOCS, SEQ, HEADS * HD)
    base_keys = jnp.clip(jax.random.normal(jax.random.fold_in(key, 11), shape, jnp.float32), -6.0, 6.0)
    base_query = jnp.clip(jax.random.normal(jax.random.fold_in(key, 12), shape, jnp.float32), -6.0, 6.0)
    return (base_query, base_keys)


def draw_query_rows(key, part):
    return pair_rows(key)[0].astype(jnp.bfloat16)


def draw_key_rows(key, part):
    return pair_rows(key)[1].astype(jnp.bfloat16)


def draw_out_grad(key, part):
    base = jnp.clip(jax.random.normal(jax.random.fold_in(key, 21), (DOCS, SEQ, D), jnp.float32), -6.0, 6.0)
    rising = 1.0 + 2.0 * jnp.arange(SEQ, dtype=jnp.float32) / SEQ
    by_doc = 1.0 + 2.0 * jnp.arange(DOCS, dtype=jnp.float32) / DOCS
    return (base * rising[None, :, None] * by_doc[:, None, None]).astype(jnp.bfloat16)


def levels(rng, dims, pieces, least, top_value):
    loudness = 1.0
    for dim, parts in pieces:
        heights = jax.random.uniform(jax.random.fold_in(jax.random.fold_in(rng, 6), dim), (parts,), jnp.float32, least / len(pieces), top_value / len(pieces))
        loudness = loudness * jnp.repeat(jnp.exp(heights), dims[dim] // parts).reshape((-1,) + (1,) * (len(dims) - 1 - dim))
    return loudness


def bell_draw(key, extent, scale, limit, pieces=(), kind=jnp.bfloat16):
    result = scale * jax.random.normal(key, extent, jnp.float32)
    if pieces:
        result = result * levels(key, extent, pieces, -0.22, 0.18)
    return jnp.clip(result, -limit, limit).astype(kind)


def setup_inputs(seed: int = 0) -> dict:
    seeds = jax.random.split(jax.random.key(seed), 8)
    return {
        "query_rows": draw_query_rows(jax.random.fold_in(seeds[7], 71), 0),
        "key_rows": draw_key_rows(jax.random.fold_in(seeds[7], 71), 0),
        "value_rows": bell_draw(seeds[2], (DOCS, SEQ, HEADS * HD), 1.0, 6.0, ((0, 64), (1, 2))),
        "prompt_keys": bell_draw(seeds[3], (DOCS, N_SEG * SUMS, HEADS * HD), 1.0, 6.0, ((0, 64), (1, 2))),
        "prompt_values": bell_draw(seeds[4], (DOCS, N_SEG * SUMS, HEADS * HD), 1.0, 6.0, ((0, 64), (1, 2))),
        "out_grad": draw_out_grad(jax.random.fold_in(seeds[7], 71), 0),
        "w_out": bell_draw(seeds[6], (HEADS * HD, D), (HEADS * HD) ** -0.5, 0.15625),
    }


def attend_back(query_seg, key_seg, value_seg, prompt_k, prompt_v, head_low, segment):
    tokens_dev = query_seg.shape[0]
    head_size = query_seg.shape[1] // HEADS
    scaling = head_size ** (-0.5)
    prefix = prompt_k.shape[0]
    keys_all = jnp.concatenate([prompt_k, key_seg], 0).astype(jnp.float32).reshape(-1, HEADS, head_size)
    values_all = jnp.concatenate([prompt_v, value_seg], 0).astype(jnp.float32).reshape(-1, HEADS, head_size)
    query_heads = query_seg.astype(jnp.float32).reshape(tokens_dev, HEADS, head_size)
    grad_heads = head_low.astype(jnp.float32).reshape(tokens_dev, HEADS, head_size)
    scores = jnp.einsum('qhd,khd->hqk', query_heads, keys_all) * scaling
    row_ids = jnp.arange(tokens_dev, dtype=jnp.int32)
    col_ids = jnp.arange(prefix + tokens_dev, dtype=jnp.int32)
    visible = jnp.where(col_ids[None, :] < prefix, (col_ids // SUMS < segment)[None, :], (col_ids - prefix)[None, :] <= row_ids[:, None])
    scores = jnp.where(visible[None], scores, jnp.float32(-1e+30))
    row_max = lax.optimization_barrier(jnp.max(scores, -1, keepdims=True))
    weights = jnp.exp(scores - row_max)
    probs = weights / lax.optimization_barrier(jnp.sum(weights, -1, keepdims=True))
    probs_low = probs.astype(jnp.bfloat16).astype(jnp.float32)
    attn = jnp.einsum('hqk,khd->qhd', probs_low, values_all).reshape(tokens_dev, -1).astype(jnp.bfloat16)
    prob_grad = jnp.einsum('qhd,khd->hqk', grad_heads, values_all)
    row_delta = lax.optimization_barrier(jnp.sum(probs * prob_grad, -1, keepdims=True))
    score_grad = (scaling * probs * (prob_grad - row_delta)).astype(jnp.bfloat16).astype(jnp.float32)
    query_grad = jnp.einsum('hqk,khd->qhd', score_grad, keys_all).reshape(tokens_dev, -1).astype(jnp.bfloat16)
    key_all_grad = jnp.einsum('hqk,qhd->khd', score_grad, query_heads).reshape(prefix + tokens_dev, -1)
    value_all_grad = jnp.einsum('hqk,qhd->khd', probs_low, grad_heads).reshape(prefix + tokens_dev, -1)
    return (query_grad, key_all_grad[prefix:].astype(jnp.bfloat16), value_all_grad[prefix:].astype(jnp.bfloat16), key_all_grad[:prefix], value_all_grad[:prefix], attn)

def reference(query_rows, key_rows, value_rows, prompt_keys, prompt_values, out_grad, w_out):
    width = query_rows.shape[2]
    head_grad = jnp.dot(out_grad.reshape(-1, D), w_out.T, preferred_element_type=jnp.float32)
    head_grad = head_grad.astype(jnp.bfloat16).reshape(DOCS, SEQ, width)

    def visit(carry, position):
        weight_acc, pk_acc, pv_acc = carry
        doc = position // N_SEG
        segment = position % N_SEG
        start = (segment * TOK).astype(jnp.int32)

        def take(array):
            return lax.dynamic_slice_in_dim(array[doc], start, TOK, 0)
        outputs = attend_back(take(query_rows), take(key_rows), take(value_rows), prompt_keys[doc], prompt_values[doc], take(head_grad), segment)
        query_grad, key_grad, value_grad, pk_part, pv_part, attn = outputs
        weight_acc = weight_acc + jnp.dot(attn.T, take(out_grad), preferred_element_type=jnp.float32)
        pk_acc = pk_acc.at[doc].add(pk_part)
        pv_acc = pv_acc.at[doc].add(pv_part)
        return ((weight_acc, pk_acc, pv_acc), (query_grad, key_grad, value_grad))
    start_carry = (jnp.zeros((width, D), jnp.float32), jnp.zeros((DOCS, N_SEG * SUMS, width), jnp.float32), jnp.zeros((DOCS, N_SEG * SUMS, width), jnp.float32))
    positions = jnp.arange(DOCS * N_SEG, dtype=jnp.int32)
    final, stacked = lax.scan(visit, start_carry, positions)
    weight_acc, pk_acc, pv_acc = final
    rms_value = jnp.sqrt(jnp.mean(weight_acc * weight_acc) + 1e-06)
    weight_grad = (weight_acc * jnp.minimum(1.0, 1.0 / rms_value)).astype(jnp.bfloat16)
    query_grad = stacked[0].reshape(DOCS, SEQ, width)
    key_grad = stacked[1].reshape(DOCS, SEQ, width)
    value_grad = stacked[2].reshape(DOCS, SEQ, width)
    return (query_grad, key_grad, value_grad, pk_acc.astype(jnp.bfloat16), pv_acc.astype(jnp.bfloat16), weight_grad)
```

```python
import functools
import math

import jax
import jax.numpy as jnp
from jax import lax
from jax.experimental import pallas as pl
from jax.experimental.pallas import tpu as pltpu
from jax.sharding import PartitionSpec as P

HEADS = 16
HD = 80
SUMS = 50
PAD = 64
TOK = 512
WIDTH = HEADS * HD
D = 2560
HALF = D // 2
QUAD = 4 * HD
WIN = 384
BLK = 256
SCALE = HD**-0.5
C2 = SCALE * math.log2(math.e)
NEG = -1e30
SIDE = 4
PLANE = SIDE * SIDE
TILES = HALF // 128
SUB = QUAD // SIDE
PIECE = SUB * TILES
STAT = 8
BF = jnp.bfloat16
F32 = jnp.float32


def dot(a, b):
    return lax.dot_general(a, b, (((1,), (0,)), ((), ())), preferred_element_type=F32)


def dot_nt(a, b):
    return lax.dot_general(a, b, (((1,), (1,)), ((), ())), preferred_element_type=F32)


def iota(shape, dim):
    return lax.broadcasted_iota(jnp.int32, shape, dim)


def fwd_kernel(
    quad, s_ref, q_hbm, k_hbm, v_hbm, pk_hbm, pv_hbm, o_ref, lse_ref, q_ref, k_ref, v_ref, pk_ref, pv_ref, vt_ref, pvt_ref, pk_in, pv_in, sem
):
    segment = s_ref[0]
    odd = quad % 2
    window = pl.ds(quad * QUAD // 128 * 128, WIN)
    pk_ref[...] = jnp.zeros_like(pk_ref)
    pv_ref[...] = jnp.zeros_like(pv_ref)
    moves = [
        pltpu.make_async_copy(src.at[:, window], dst, sem.at[n])
        for n, (src, dst) in enumerate(
            (
                (q_hbm, q_ref),
                (k_hbm, k_ref),
                (pk_hbm, pk_in),
                (v_hbm, v_ref),
                (pv_hbm, pv_in),
            )
        )
    ]
    for move in moves:
        move.start()
    for move in moves[:3]:
        move.wait()
    pk_ref[:SUMS] = pk_in[...]
    for move in moves[3:]:
        move.wait()
    pv_ref[:SUMS] = pv_in[...]
    vt_ref[...] = jnp.transpose(v_ref[...])
    pvt_ref[...] = jnp.transpose(pv_ref[...])
    lanes = iota((TOK, BLK), 1)
    causal = iota((BLK, BLK), 0) <= iota((BLK, BLK), 1)
    seen = iota((PAD, TOK), 0) < SUMS * segment
    for h in range(4):
        at = 0 if h < 2 else 128
        low = 64 * odd + HD * h - at
        mine = (lanes >= low) & (lanes < low + HD)
        qm = jnp.where(mine, q_ref[:, at : at + BLK], jnp.zeros((), BF))
        s0 = dot_nt(k_ref[:BLK, at : at + BLK], qm)
        s1 = dot_nt(k_ref[BLK:, at : at + BLK], qm[BLK:])
        sp = jnp.where(seen, dot_nt(pk_ref[:, at : at + BLK], qm), NEG)
        s00 = jnp.where(causal, s0[:, :BLK], NEG)
        s01 = s0[:, BLK:]
        s11 = jnp.where(causal, s1, NEG)
        mp = jnp.max(sp, 0, keepdims=True)
        m0 = jnp.maximum(jnp.max(s00, 0, keepdims=True), mp[:, :BLK])
        m1 = jnp.maximum(
            jnp.maximum(jnp.max(s01, 0, keepdims=True), jnp.max(s11, 0, keepdims=True)), mp[:, BLK:]
        )
        e00 = jnp.exp2((s00 - m0) * C2)
        e01 = jnp.exp2((s01 - m1) * C2)
        e11 = jnp.exp2((s11 - m1) * C2)
        ep0 = jnp.exp2((sp[:, :BLK] - m0) * C2)
        ep1 = jnp.exp2((sp[:, BLK:] - m1) * C2)
        l0 = jnp.sum(e00, 0, keepdims=True) + jnp.sum(ep0, 0, keepdims=True)
        l1 = (
            jnp.sum(e01, 0, keepdims=True)
            + jnp.sum(e11, 0, keepdims=True)
            + jnp.sum(ep1, 0, keepdims=True)
        )
        row = slice(64 * odd + HD * h, 64 * odd + HD * h + HD)
        vt = vt_ref[row, :]
        pvt = pvt_ref[row, :]
        o0 = dot(vt[:, :BLK], e00.astype(BF)) + dot(pvt, ep0.astype(BF))
        o1 = (
            dot(vt[:, :BLK], e01.astype(BF))
            + dot(vt[:, BLK:], e11.astype(BF))
            + dot(pvt, ep1.astype(BF))
        )
        o_ref[HD * h : HD * h + HD, :BLK] = (o0 / l0).astype(BF)
        o_ref[HD * h : HD * h + HD, BLK:] = (o1 / l1).astype(BF)
        lse_ref[h : h + 1, :BLK] = m0 * C2 + jnp.log2(l0)
        lse_ref[h : h + 1, BLK:] = m1 * C2 + jnp.log2(l1)


def forward_quad(quad, scalars, q, k, v, pk, pv):
    any_spec = pl.BlockSpec(memory_space=pltpu.HBM)
    return pl.pallas_call(
        functools.partial(fwd_kernel, quad),
        out_shape=(
            jax.ShapeDtypeStruct((QUAD, TOK), BF),
            jax.ShapeDtypeStruct((4, TOK), F32),
        ),
        grid_spec=pltpu.PrefetchScalarGridSpec(
            num_scalar_prefetch=1,
            grid=(1,),
            in_specs=[any_spec] * 5,
            out_specs=(
                pl.BlockSpec((QUAD, TOK), lambda i, s: (0, 0)),
                pl.BlockSpec((4, TOK), lambda i, s: (0, 0)),
            ),
            scratch_shapes=[
                pltpu.VMEM((TOK, WIN), BF),
                pltpu.VMEM((TOK, WIN), BF),
                pltpu.VMEM((TOK, WIN), BF),
                pltpu.VMEM((PAD, WIN), BF),
                pltpu.VMEM((PAD, WIN), BF),
                pltpu.VMEM((WIN, TOK), BF),
                pltpu.VMEM((WIN, PAD), BF),
                pltpu.VMEM((SUMS, WIN), BF),
                pltpu.VMEM((SUMS, WIN), BF),
                pltpu.SemaphoreType.DMA((5,)),
            ],
        ),
        compiler_params=pltpu.CompilerParams(vmem_limit_bytes=24 << 20),
        cost_estimate=pl.CostEstimate(
            flops=4 * 2 * 2 * 896 * 256 * 256, transcendentals=4 * 896 * 256, bytes_accessed=1600000
        ),
        name="fwd_quad",
    )(scalars, q, k, v, pk, pv)


def bwd_kernel(
    pair, s_ref, q_ref, k_ref, v_ref, g_ref, pk_in, pv_in, lse_a, lse_b, *rest
):
    dq_ref, dk_ref, dv_ref, dpk_ref, dpv_ref = rest[-14:-9]
    kt_ref, pkt_ref, dqt_ref, dka_ref, dva_ref, dpka_ref, dpva_ref, pk_ref, pv_ref = rest[-9:]
    segment = s_ref[0]
    pk_ref[...] = jnp.zeros_like(pk_ref)
    pv_ref[...] = jnp.zeros_like(pv_ref)
    pk_ref[:SUMS] = pk_in[...]
    pv_ref[:SUMS] = pv_in[...]
    kt_ref[...] = jnp.transpose(k_ref[...])
    pkt_ref[...] = jnp.transpose(pk_ref[...])
    for acc in (dka_ref, dva_ref, dpka_ref, dpva_ref):
        acc[...] = jnp.zeros_like(acc)
    causal = iota((BLK, BLK), 0) <= iota((BLK, BLK), 1)
    seen = iota((PAD, TOK), 0) < SUMS * segment
    for h in range(8):
        low = HD * h
        at = low // 128 * 128
        wide = 128 if low - at + HD <= 128 else 256
        w = slice(at, at + wide)
        lanes = iota((TOK, wide), 1) + at
        mine = (lanes >= low) & (lanes < low + HD)
        qm = jnp.where(mine, q_ref[:, w], jnp.zeros((), BF))
        gm = jnp.where(mine, g_ref[:, w], jnp.zeros((), BF))
        lse = (lse_a, lse_b)[h // 4][h % 4 : h % 4 + 1, :]
        lse0, lse1 = lse[:, :BLK], lse[:, BLK:]
        s0 = dot_nt(k_ref[:BLK, w], qm)
        s1 = dot_nt(k_ref[BLK:, w], qm[BLK:])
        sp = dot_nt(pk_ref[:, w], qm)
        p00 = jnp.exp2(jnp.where(causal, s0[:, :BLK] * C2 - lse0, NEG))
        p01 = jnp.exp2(s0[:, BLK:] * C2 - lse1)
        p11 = jnp.exp2(jnp.where(causal, s1 * C2 - lse1, NEG))
        pp = jnp.exp2(jnp.where(seen, sp * C2 - lse, NEG))
        d0 = dot_nt(v_ref[:BLK, w], gm)
        d11 = dot_nt(v_ref[BLK:, w], gm[BLK:])
        dp = dot_nt(pv_ref[:, w], gm)
        d00, d01 = d0[:, :BLK], d0[:, BLK:]
        deltap = jnp.sum(pp * dp, 0, keepdims=True)
        delta0 = jnp.sum(p00 * d00, 0, keepdims=True) + deltap[:, :BLK]
        delta1 = (
            jnp.sum(p01 * d01, 0, keepdims=True)
            + jnp.sum(p11 * d11, 0, keepdims=True)
            + deltap[:, BLK:]
        )
        delta = jnp.concatenate([delta0, delta1], 1)
        t00 = (p00 * (d00 - delta0) * SCALE).astype(BF)
        t01 = (p01 * (d01 - delta1) * SCALE).astype(BF)
        t11 = (p11 * (d11 - delta1) * SCALE).astype(BF)
        tp = (pp * (dp - delta) * SCALE).astype(BF)
        t0 = jnp.concatenate([t00, t01], 1)
        row = slice(low, low + HD)
        dqt = dot(kt_ref[row, :BLK], t0) + dot(pkt_ref[row, :], tp)
        dqt_ref[row, :BLK] = dqt[:, :BLK].astype(BF)
        dqt_ref[row, BLK:] = (dqt[:, BLK:] + dot(kt_ref[row, BLK:], t11)).astype(BF)
        dka_ref[:BLK, w] += dot(t0, qm)
        dka_ref[BLK:, w] += dot(t11, qm[BLK:])
        dpka_ref[:, w] += dot(tp, qm)
        low0 = jnp.concatenate([p00.astype(BF), p01.astype(BF)], 1)
        dva_ref[:BLK, w] += dot(low0, gm)
        dva_ref[BLK:, w] += dot(p11.astype(BF), gm[BLK:])
        dpva_ref[:, w] += dot(pp.astype(BF), gm)
    dq_ref[...] = jnp.transpose(dqt_ref[...])
    dk_ref[...] = dka_ref[...].astype(BF)
    dv_ref[...] = dva_ref[...].astype(BF)
    dpk_ref[...] = dpka_ref[:SUMS].astype(BF)
    dpv_ref[...] = dpva_ref[:SUMS].astype(BF)


def backward_pair(pair, scalars, q, k, v, g, pk, pv, lses, before=()):
    wide = 8 * HD
    rows = pl.BlockSpec((TOK, wide), lambda i, s: (0, pair))
    prompt = pl.BlockSpec((SUMS, wide), lambda i, s: (0, pair))
    return pl.pallas_call(
        functools.partial(bwd_kernel, pair),
        out_shape=(jax.ShapeDtypeStruct((TOK, WIDTH), BF),) * 3
        + (jax.ShapeDtypeStruct((SUMS, WIDTH), BF),) * 2,
        grid_spec=pltpu.PrefetchScalarGridSpec(
            num_scalar_prefetch=1,
            grid=(1,),
            in_specs=[rows] * 4
            + [prompt] * 2
            + [pl.BlockSpec((4, TOK), lambda i, s: (0, 0))] * 2
            + [pl.BlockSpec(memory_space=pl.ANY)] * len(before),
            out_specs=(rows, rows, rows, prompt, prompt),
            scratch_shapes=[
                pltpu.VMEM((wide, TOK), BF),
                pltpu.VMEM((wide, PAD), BF),
                pltpu.VMEM((wide, TOK), BF),
                pltpu.VMEM((TOK, wide), F32),
                pltpu.VMEM((TOK, wide), F32),
                pltpu.VMEM((PAD, wide), F32),
                pltpu.VMEM((PAD, wide), F32),
                pltpu.VMEM((PAD, wide), BF),
                pltpu.VMEM((PAD, wide), BF),
            ],
        ),
        input_output_aliases={9 + n: n for n in range(len(before))},
        compiler_params=pltpu.CompilerParams(vmem_limit_bytes=40 << 20),
        cost_estimate=pl.CostEstimate(
            flops=8 * 5 * 2 * 896 * 256 * 256, transcendentals=8 * 896 * 256, bytes_accessed=5000000
        ),
        name=f"attend_back_{pair}",
    )(scalars, q, k, v, g, pk, pv, *lses[2 * pair : 2 * pair + 2], *before)


WCOLS = 640


def weight_kernel(bys, s_ref, *refs):
    owns, others, g_ref, h_ref = refs[:SIDE], refs[SIDE : 2 * SIDE], refs[2 * SIDE], refs[2 * SIDE + 1]
    outs, picked = refs[2 * SIDE + 2 : -1], refs[-1]
    for n, by in enumerate(bys):
        quad = (s_ref[1] + by) % SIDE
        for j in range(SIDE):

            @pl.when((pl.program_id(0) == 0) & (quad == j))
            def _():
                picked[n, 0] = owns[j][...]
                picked[n, 1] = others[j][...]

    for n, out_ref in enumerate(outs):
        out = dot(picked[n, 0], g_ref[...]) + dot(picked[n, 1], h_ref[...])
        for sub in range(SIDE):
            for tile in range(WCOLS // 128):
                out_ref[sub, tile] = out[sub * SUB : sub * SUB + SUB, tile * 128 : tile * 128 + 128].astype(
                    out_ref.dtype
                )


def weight_quads(bys, scalars, owns, others, grad_rows, grad_other):
    count = len(bys)
    quad = pl.BlockSpec((QUAD, TOK), lambda n, s: (0, 0))
    columns = pl.BlockSpec((TOK, WCOLS), lambda n, s: (0, n + s[0] * (HALF // WCOLS)))
    outs = pl.pallas_call(
        functools.partial(weight_kernel, bys),
        out_shape=[jax.ShapeDtypeStruct((SIDE, TILES, SUB, 128), BF if by else F32) for by in bys],
        grid_spec=pltpu.PrefetchScalarGridSpec(
            num_scalar_prefetch=1,
            grid=(HALF // WCOLS,),
            in_specs=[quad] * (2 * SIDE) + [columns, columns],
            out_specs=[pl.BlockSpec((SIDE, WCOLS // 128, SUB, 128), lambda n, s: (0, n, 0, 0))] * count,
            scratch_shapes=[pltpu.VMEM((count, 2, QUAD, TOK), BF)],
        ),
        compiler_params=pltpu.CompilerParams(vmem_limit_bytes=24 << 20),
        cost_estimate=pl.CostEstimate(
            flops=count * 4 * QUAD * TOK * HALF, transcendentals=0, bytes_accessed=4200000
        ),
        name="weight_quads",
    )(scalars, *owns, *others, grad_rows, grad_other)
    return [out.reshape(SIDE, PIECE, 128) for out in outs]


def line_kernel(s_ref, own, r1, r2, r3, o0, o1, o2, o3):
    total = (own[0] + r2[0].astype(F32)) + (r1[0].astype(F32) + r3[0].astype(F32))
    for by, out in enumerate((o0, o1, o2, o3)):

        @pl.when(pl.program_id(0) == by)
        def _():
            out[...] = total.astype(out.dtype)


def sum_line(scalars, own, r1, r2, r3):
    block = pl.BlockSpec((1, PIECE, 128), lambda n, s: ((s[2] + n) % SIDE, 0, 0))
    whole = pl.BlockSpec((PIECE, 128), lambda n, s: (0, 0))
    return pl.pallas_call(
        line_kernel,
        out_shape=[jax.ShapeDtypeStruct((PIECE, 128), kind) for kind in (F32, BF, BF, BF)],
        grid_spec=pltpu.PrefetchScalarGridSpec(
            num_scalar_prefetch=1, grid=(SIDE,), in_specs=[block] * 4, out_specs=[whole] * 4
        ),
        compiler_params=pltpu.CompilerParams(vmem_limit_bytes=16 << 20),
        cost_estimate=pl.CostEstimate(flops=2000000, transcendentals=0, bytes_accessed=5000000),
        name="sum_line",
    )(scalars, own, r1, r2, r3)


def mid_kernel(own, r1, r2, r3, out):
    total = (own[...] + r2[...].astype(F32)) + (r1[...].astype(F32) + r3[...].astype(F32))
    out[...] = total.astype(BF)


def sum_mid(own, r1, r2, r3):
    return pl.pallas_call(
        mid_kernel,
        out_shape=jax.ShapeDtypeStruct((PIECE, 128), BF),
        compiler_params=pltpu.CompilerParams(vmem_limit_bytes=8 << 20),
        cost_estimate=pl.CostEstimate(flops=400000, transcendentals=0, bytes_accessed=1200000),
        name="sum_mid",
    )(own, r1, r2, r3)


def cross_kernel(own, r1, r2, r3, out):
    total = (own[...].astype(F32) + r2[...].astype(F32)) + (r1[...].astype(F32) + r3[...].astype(F32))
    out[:PIECE] = total.astype(BF)
    square = jnp.sum(total * total, 0, keepdims=True)
    terms = split_three(square)
    out[PIECE:] = jnp.concatenate(terms + (jnp.zeros((STAT - 3, 128), BF),), 0)


def sum_cross(own, r1, r2, r3):
    return pl.pallas_call(
        cross_kernel,
        out_shape=jax.ShapeDtypeStruct((PIECE + STAT, 128), BF),
        compiler_params=pltpu.CompilerParams(vmem_limit_bytes=8 << 20),
        cost_estimate=pl.CostEstimate(flops=600000, transcendentals=0, bytes_accessed=1200000),
        name="sum_cross",
    )(own, r1, r2, r3)


def split_three(x):
    high = x.astype(BF)
    rest = x - high.astype(F32)
    mid = rest.astype(BF)
    return high, mid, (rest - mid.astype(F32)).astype(BF)


def final_kernel(s_ref, *refs):
    pieces, out_hbm, bufs, outs, sem, out_sem = refs[:8], refs[8], refs[9], refs[10], refs[11], refs[12]
    segment, x, y, z = s_ref[0], s_ref[3], s_ref[4], s_ref[5]
    moves = [pltpu.make_async_copy(pieces[n], bufs.at[n], sem.at[n]) for n in range(8)]
    for move in moves:
        move.start()
    total = jnp.zeros((1, 128), F32)
    for n in range(8):
        moves[n].wait()
        for p in range(SIDE):
            stat = bufs[n, p, PIECE : PIECE + STAT, :].astype(F32)
            total = total + jnp.sum(stat, 0, keepdims=True)
    mean = jnp.sum(total, 1, keepdims=True) * (1.0 / (WIDTH * D))
    scale = jnp.minimum(1.0, 1.0 / jnp.sqrt(mean + 1e-06))
    writes = []
    for n in range(8):
        k = n % 4
        half = segment if n < 4 else 1 - segment
        quad = (jnp.where(half == 0, x, y) + SIDE - k) % SIDE
        at = jnp.where(half == 0, z, x)
        for p in range(SIDE):
            rows = pl.ds(pl.multiple_of((at + SIDE - p) % SIDE * SUB, 16), SUB)
            for tile in range(TILES):
                outs[n, rows, tile * 128 : tile * 128 + 128] = (
                    bufs[n, p, tile * SUB : tile * SUB + SUB, :].astype(F32) * scale
                ).astype(BF)
        write = pltpu.make_async_copy(
            outs.at[n],
            out_hbm.at[
                pl.ds(pl.multiple_of(quad * QUAD, 64), QUAD), pl.ds(pl.multiple_of(half * HALF, 128), HALF)
            ],
            out_sem.at[n],
        )
        write.start()
        writes.append(write)
    for write in writes:
        write.wait()


def finish(scalars, pieces):
    any_spec = pl.BlockSpec(memory_space=pl.ANY)
    return pl.pallas_call(
        final_kernel,
        out_shape=jax.ShapeDtypeStruct((WIDTH, D), BF),
        grid_spec=pltpu.PrefetchScalarGridSpec(
            num_scalar_prefetch=1,
            grid=(1,),
            in_specs=[any_spec] * 8,
            out_specs=any_spec,
            scratch_shapes=[
                pltpu.VMEM((8, SIDE, PIECE + STAT, 128), BF),
                pltpu.VMEM((8, QUAD, HALF), BF),
                pltpu.SemaphoreType.DMA((8,)),
                pltpu.SemaphoreType.DMA((8,)),
            ],
        ),
        compiler_params=pltpu.CompilerParams(vmem_limit_bytes=32 << 20),
        cost_estimate=pl.CostEstimate(flops=7000000, transcendentals=0, bytes_accessed=14000000),
        name="clip",
    )(scalars, *pieces)


def step(chip, axis, by):
    stride = {"x": 1, "y": SIDE, "z": SIDE * SIDE}[axis]
    at = (chip // stride) % SIDE
    return chip + (((at + by) % SIDE) - at) * stride


CHIPS = SIDE**3


def along(first, second, by):
    return [(c, step(c, first, by)) for c in range(CHIPS)] + [
        (CHIPS + c, CHIPS + step(c, second, by)) for c in range(CHIPS)
    ]


BOTH = ("seg", "dp")
SWAP = [(0, 1), (1, 0)]


def shards(query_rows, key_rows, value_rows, prompt_keys, prompt_values, out_grad, w_out):
    segment = lax.axis_index("seg")
    chip = lax.axis_index("dp")
    x, y, z = chip % SIDE, (chip // SIDE) % SIDE, chip // PLANE
    turn = jnp.where(segment == 0, x, y)
    sub = jnp.where(segment == 0, z, x)
    scalars = jnp.stack([segment, turn, sub, x, y, z]).astype(jnp.int32)
    q, k, v, grad_rows = query_rows[0], key_rows[0], value_rows[0], out_grad[0]

    pk = lax.ppermute(prompt_keys[0], "seg", [(0, 1)])
    pv = lax.ppermute(prompt_values[0], "seg", [(0, 1)])
    grad_other = lax.ppermute(grad_rows, "seg", SWAP)

    attn, other, lses, parts = {}, {}, {}, {}
    for quad in range(SIDE):
        attn[quad], lses[quad] = forward_quad(quad, scalars, q, k, v, pk, pv)
        other[quad] = lax.ppermute(attn[quad], "seg", SWAP)
    owns, others, lses = ([d[quad] for quad in range(SIDE)] for d in (attn, other, lses))
    for bys in WEIGHT_GROUPS:
        parts.update(zip(bys, weight_quads(bys, scalars, owns, others, grad_rows, grad_other)))
    sent = {by: lax.ppermute(parts[by], BOTH, along("x", "y", by)) for by in (2, 1, 3)}

    head_low = jnp.einsum("td,hd->th", grad_rows, w_out, preferred_element_type=F32).astype(BF)
    back = backward_pair(0, scalars, q, k, v, head_low, pk, pv, lses)
    sent, back = lax.optimization_barrier((sent, back))
    own, *rest = sum_line(scalars, parts[0], sent[1], sent[2], sent[3])
    own = sum_mid(own, *[lax.ppermute(rest[by - 1], BOTH, along("z", "x", by)) for by in (1, 2, 3)])
    own = sum_cross(own, *[lax.ppermute(own, BOTH, along("y", "z", by)) for by in (1, 2, 3)])
    own = jnp.stack([own] + [lax.ppermute(own, BOTH, along("z", "x", by)) for by in (1, 2, 3)])

    own, back = lax.optimization_barrier((own, back))
    pieces = [lax.ppermute(own, BOTH, along("x", "y", by)) for by in (1, 2, 3)]
    back = backward_pair(1, scalars, q, k, v, head_low, pk, pv, lses, back)
    pieces, back = lax.optimization_barrier((pieces, back))
    dq, dk, dv, dpk, dpv = back
    dpk = lax.ppermute(dpk, "seg", [(1, 0)])
    dpv = lax.ppermute(dpv, "seg", [(1, 0)])
    pieces = [own] + pieces
    pieces = pieces + [lax.ppermute(part, "seg", SWAP) for part in pieces]
    weight_grad = finish(scalars, pieces)
    return (dq[None], dk[None], dv[None], dpk[None], dpv[None], weight_grad)


WEIGHT_GROUPS = ((2, 1), (3, 0))


def solution(mesh):
    rows = P("dp", "seg", None)
    return jax.shard_map(
        shards,
        mesh=mesh,
        in_specs=(rows,) * 6 + (P(),),
        out_specs=(rows,) * 5 + (P(),),
        check_vma=False,
    )
```

```python
import functools
import math

import jax
import jax.numpy as jnp
from jax import lax
from jax.experimental import pallas as pl
from jax.experimental.pallas import tpu as pltpu
from jax.sharding import PartitionSpec as P


HEADS = 16
HD = 80
SUMS = 50
PAD = 64
TOK = 512
WIDTH = HEADS * HD
D = 2560
HALF = D // 2
QUAD = 4 * HD
WIN = 384
BLK = 256
SCALE = HD**-0.5
C2 = SCALE * math.log2(math.e)
NEG = -1e30
SIDE = 4
TILES = HALF // 128
SUB = QUAD // SIDE
PIECE = SUB * TILES
STAT = 8
ORDER = 6
BF = jnp.bfloat16
F32 = jnp.float32


def dot(a, b):
    return lax.dot_general(a, b, (((1,), (0,)), ((), ())), preferred_element_type=F32)


def dot_nt(a, b):
    return lax.dot_general(a, b, (((1,), (1,)), ((), ())), preferred_element_type=F32)


def iota(shape, dim):
    return lax.broadcasted_iota(jnp.int32, shape, dim)


def fwd_kernel(place, s_ref, q_hbm, k_hbm, v_hbm, pk_hbm, pv_hbm, *rest):
    o_ref, lse_ref, q_ref, k_ref, v_ref, pk_ref, pv_ref, vt_ref, pvt_ref, pk_in, pv_in, sem = rest[-12:]
    segment = s_ref[0]
    quad = s_ref[ORDER + place]
    odd = quad & 1
    window = pl.ds(pl.multiple_of(((quad * 5) >> 1) * 128, 128), WIN)
    pk_ref[...] = jnp.zeros_like(pk_ref)
    pv_ref[...] = jnp.zeros_like(pv_ref)
    moves = [
        pltpu.make_async_copy(src.at[:, window], dst, sem.at[n])
        for n, (src, dst) in enumerate(
            (
                (q_hbm, q_ref),
                (k_hbm, k_ref),
                (pk_hbm, pk_in),
                (v_hbm, v_ref),
                (pv_hbm, pv_in),
            )
        )
    ]
    for move in moves:
        move.start()
    for move in moves[:3]:
        move.wait()
    pk_ref[:SUMS] = pk_in[...]
    for move in moves[3:]:
        move.wait()
    pv_ref[:SUMS] = pv_in[...]
    vt_ref[...] = jnp.transpose(v_ref[...])
    pvt_ref[...] = jnp.transpose(pv_ref[...])
    lanes = iota((TOK, BLK), 1)
    causal = iota((BLK, BLK), 0) <= iota((BLK, BLK), 1)
    seen = iota((PAD, TOK), 0) < SUMS * segment

    def head(h, at):
        low = 64 * odd + HD * h - at
        w = pl.ds(at, BLK)
        mine = (lanes >= low) & (lanes < low + HD)
        qm = jnp.where(mine, q_ref[:, w], jnp.zeros((), BF))
        s0 = dot_nt(k_ref[:BLK, w], qm)
        s1 = dot_nt(k_ref[BLK:, w], qm[BLK:])
        sp = jnp.where(seen, dot_nt(pk_ref[:, w], qm), NEG)
        s00 = jnp.where(causal, s0[:, :BLK], NEG)
        s01 = s0[:, BLK:]
        s11 = jnp.where(causal, s1, NEG)
        mp = jnp.max(sp, 0, keepdims=True)
        m0 = jnp.maximum(jnp.max(s00, 0, keepdims=True), mp[:, :BLK])
        m1 = jnp.maximum(
            jnp.maximum(jnp.max(s01, 0, keepdims=True), jnp.max(s11, 0, keepdims=True)), mp[:, BLK:]
        )
        e00 = jnp.exp2((s00 - m0) * C2)
        e01 = jnp.exp2((s01 - m1) * C2)
        e11 = jnp.exp2((s11 - m1) * C2)
        ep0 = jnp.exp2((sp[:, :BLK] - m0) * C2)
        ep1 = jnp.exp2((sp[:, BLK:] - m1) * C2)
        l0 = jnp.sum(e00, 0, keepdims=True) + jnp.sum(ep0, 0, keepdims=True)
        l1 = (
            jnp.sum(e01, 0, keepdims=True)
            + jnp.sum(e11, 0, keepdims=True)
            + jnp.sum(ep1, 0, keepdims=True)
        )
        row = pl.ds(pl.multiple_of(64 * odd + HD * h, 16), HD)
        to = slice(HD * h, HD * h + HD)
        vt = vt_ref[row, :]
        pvt = pvt_ref[row, :]
        o0 = dot(vt[:, :BLK], e00.astype(BF)) + dot(pvt, ep0.astype(BF))
        o1 = (
            dot(vt[:, :BLK], e01.astype(BF))
            + dot(vt[:, BLK:], e11.astype(BF))
            + dot(pvt, ep1.astype(BF))
        )
        o_ref[to, :BLK] = (o0 / l0).astype(BF)
        o_ref[to, BLK:] = (o1 / l1).astype(BF)
        lse_ref[pl.ds(h, 1), :BLK] = m0 * C2 + jnp.log2(l0)
        lse_ref[pl.ds(h, 1), BLK:] = m1 * C2 + jnp.log2(l1)

    for h in range(4):
        head(h, h // 2 * 128)


def forward_quad(place, scalars, q, k, v, pk, pv, after):
    any_spec = pl.BlockSpec(memory_space=pl.ANY)
    return pl.pallas_call(
        functools.partial(fwd_kernel, place),
        out_shape=(
            jax.ShapeDtypeStruct((QUAD, TOK), BF),
            jax.ShapeDtypeStruct((4, TOK), F32),
        ),
        grid_spec=pltpu.PrefetchScalarGridSpec(
            num_scalar_prefetch=1,
            grid=(1,),
            in_specs=[any_spec] * (5 + len(after)),
            out_specs=(
                pl.BlockSpec((QUAD, TOK), lambda i, s: (0, 0)),
                pl.BlockSpec((4, TOK), lambda i, s: (0, 0)),
            ),
            scratch_shapes=[
                pltpu.VMEM((TOK, WIN), BF),
                pltpu.VMEM((TOK, WIN), BF),
                pltpu.VMEM((TOK, WIN), BF),
                pltpu.VMEM((PAD, WIN), BF),
                pltpu.VMEM((PAD, WIN), BF),
                pltpu.VMEM((WIN, TOK), BF),
                pltpu.VMEM((WIN, PAD), BF),
                pltpu.VMEM((SUMS, WIN), BF),
                pltpu.VMEM((SUMS, WIN), BF),
                pltpu.SemaphoreType.DMA((5,)),
            ],
        ),
        compiler_params=pltpu.CompilerParams(vmem_limit_bytes=24 << 20),
        cost_estimate=pl.CostEstimate(
            flops=4 * 2 * 2 * 896 * 256 * 256, transcendentals=4 * 896 * 256, bytes_accessed=1600000
        ),
        name="fwd_quad",
    )(scalars, q, k, v, pk, pv, *after)


def bwd_kernel(
    s_ref, q_ref, k_ref, v_ref, g_ref, pk_in, pv_in, lse_0, lse_1, lse_2, lse_3,
    dq_ref, dk_ref, dv_ref, dp_ref,
    kt_ref, pkt_ref, dqt_ref, dka_ref, dva_ref, dpka_ref, dpva_ref, pk_ref, pv_ref, lse_ref,
):
    for n in range(2):
        lse = lse_0[...]
        for place, other in ((1, lse_1), (2, lse_2), (3, lse_3)):
            lse = jnp.where(s_ref[ORDER + place] == 2 * pl.program_id(0) + n, other[...], lse)
        lse_ref[4 * n : 4 * n + 4] = lse
    segment = s_ref[0]
    pk_ref[...] = jnp.zeros_like(pk_ref)
    pv_ref[...] = jnp.zeros_like(pv_ref)
    pk_ref[:SUMS] = pk_in[...]
    pv_ref[:SUMS] = pv_in[...]
    kt_ref[...] = jnp.transpose(k_ref[...])
    pkt_ref[...] = jnp.transpose(pk_ref[...])
    for acc in (dka_ref, dva_ref, dpka_ref, dpva_ref):
        acc[...] = jnp.zeros_like(acc)
    causal = iota((BLK, BLK), 0) <= iota((BLK, BLK), 1)
    seen = iota((PAD, TOK), 0) < SUMS * segment
    for h in range(8):
        low = HD * h
        at = low // 128 * 128
        wide = 128 if low - at + HD <= 128 else 256
        w = slice(at, at + wide)
        lanes = iota((TOK, wide), 1) + at
        mine = (lanes >= low) & (lanes < low + HD)
        qm = jnp.where(mine, q_ref[:, w], jnp.zeros((), BF))
        gm = jnp.where(mine, g_ref[:, w], jnp.zeros((), BF))
        lse = lse_ref[h : h + 1, :]
        lse0, lse1 = lse[:, :BLK], lse[:, BLK:]
        s0 = dot_nt(k_ref[:BLK, w], qm)
        s1 = dot_nt(k_ref[BLK:, w], qm[BLK:])
        sp = dot_nt(pk_ref[:, w], qm)
        p00 = jnp.exp2(jnp.where(causal, s0[:, :BLK] * C2 - lse0, NEG))
        p01 = jnp.exp2(s0[:, BLK:] * C2 - lse1)
        p11 = jnp.exp2(jnp.where(causal, s1 * C2 - lse1, NEG))
        pp = jnp.exp2(jnp.where(seen, sp * C2 - lse, NEG))
        d0 = dot_nt(v_ref[:BLK, w], gm)
        d11 = dot_nt(v_ref[BLK:, w], gm[BLK:])
        dp = dot_nt(pv_ref[:, w], gm)
        d00, d01 = d0[:, :BLK], d0[:, BLK:]
        deltap = jnp.sum(pp * dp, 0, keepdims=True)
        delta0 = jnp.sum(p00 * d00, 0, keepdims=True) + deltap[:, :BLK]
        delta1 = (
            jnp.sum(p01 * d01, 0, keepdims=True)
            + jnp.sum(p11 * d11, 0, keepdims=True)
            + deltap[:, BLK:]
        )
        delta = jnp.concatenate([delta0, delta1], 1)
        t00 = (p00 * (d00 - delta0) * SCALE).astype(BF)
        t01 = (p01 * (d01 - delta1) * SCALE).astype(BF)
        t11 = (p11 * (d11 - delta1) * SCALE).astype(BF)
        tp = (pp * (dp - delta) * SCALE).astype(BF)
        t0 = jnp.concatenate([t00, t01], 1)
        row = slice(low, low + HD)
        dqt = dot(kt_ref[row, :BLK], t0) + dot(pkt_ref[row, :], tp)
        dqt_ref[row, :BLK] = dqt[:, :BLK].astype(BF)
        dqt_ref[row, BLK:] = (dqt[:, BLK:] + dot(kt_ref[row, BLK:], t11)).astype(BF)
        dka_ref[:BLK, w] += dot(t0, qm)
        dka_ref[BLK:, w] += dot(t11, qm[BLK:])
        dpka_ref[:, w] += dot(tp, qm)
        low0 = jnp.concatenate([p00.astype(BF), p01.astype(BF)], 1)
        dva_ref[:BLK, w] += dot(low0, gm)
        dva_ref[BLK:, w] += dot(p11.astype(BF), gm[BLK:])
        dpva_ref[:, w] += dot(pp.astype(BF), gm)
    dq_ref[...] = jnp.transpose(dqt_ref[...])
    dk_ref[...] = dka_ref[...].astype(BF)
    dv_ref[...] = dva_ref[...].astype(BF)
    dp_ref[0] = dpka_ref[:SUMS].astype(BF)
    dp_ref[1] = dpva_ref[:SUMS].astype(BF)


def backward(scalars, q, k, v, g, pk, pv, lses):
    wide = 8 * HD
    rows = pl.BlockSpec((TOK, wide), lambda i, s: (0, i))
    prompt = pl.BlockSpec((SUMS, wide), lambda i, s: (0, i))
    return pl.pallas_call(
        bwd_kernel,
        out_shape=(jax.ShapeDtypeStruct((TOK, WIDTH), BF),) * 3
        + (jax.ShapeDtypeStruct((2, SUMS, WIDTH), BF),),
        grid_spec=pltpu.PrefetchScalarGridSpec(
            num_scalar_prefetch=1,
            grid=(2,),
            in_specs=[rows] * 4 + [prompt] * 2 + [pl.BlockSpec((4, TOK), lambda i, s: (0, 0))] * 4,
            out_specs=(rows, rows, rows, pl.BlockSpec((2, SUMS, wide), lambda i, s: (0, 0, i))),
            scratch_shapes=[
                pltpu.VMEM((wide, TOK), BF),
                pltpu.VMEM((wide, PAD), BF),
                pltpu.VMEM((wide, TOK), BF),
                pltpu.VMEM((TOK, wide), F32),
                pltpu.VMEM((TOK, wide), F32),
                pltpu.VMEM((PAD, wide), F32),
                pltpu.VMEM((PAD, wide), F32),
                pltpu.VMEM((PAD, wide), BF),
                pltpu.VMEM((PAD, wide), BF),
                pltpu.VMEM((8, TOK), F32),
            ],
        ),
        compiler_params=pltpu.CompilerParams(vmem_limit_bytes=36 << 20),
        cost_estimate=pl.CostEstimate(
            flops=16 * 5 * 2 * 896 * 256 * 256, transcendentals=16 * 896 * 256, bytes_accessed=10000000
        ),
        name="attend_back",
    )(scalars, q, k, v, g, pk, pv, *lses)


WCOLS = 640


def weight_kernel(bys, places, s_ref, *refs):
    owns, others, g_ref, h_ref = refs[:places], refs[places : 2 * places], refs[2 * places], refs[2 * places + 1]
    outs, picked = refs[2 * places + 2 : -1], refs[-1]
    for n, by in enumerate(bys):
        quad = (s_ref[1] + by) & (SIDE - 1)
        for j in range(places):

            @pl.when((pl.program_id(0) == 0) & (quad == s_ref[ORDER + j]))
            def _():
                picked[n, 0] = owns[j][...]
                picked[n, 1] = others[j][...]

    for n, out_ref in enumerate(outs):
        out = dot(picked[n, 0], g_ref[...]) + dot(picked[n, 1], h_ref[...])
        for sub in range(SIDE):
            for tile in range(WCOLS // 128):
                out_ref[sub, tile] = out[sub * SUB : sub * SUB + SUB, tile * 128 : tile * 128 + 128].astype(
                    out_ref.dtype
                )


def weight_quads(bys, scalars, owns, others, grad_rows, grad_other):
    count, places = len(bys), len(owns)
    quad = pl.BlockSpec((QUAD, TOK), lambda n, s: (0, 0))
    columns = pl.BlockSpec((TOK, WCOLS), lambda n, s: (0, n + s[0] * (HALF // WCOLS)))
    outs = pl.pallas_call(
        functools.partial(weight_kernel, bys, places),
        out_shape=[jax.ShapeDtypeStruct((SIDE, TILES, SUB, 128), BF if by else F32) for by in bys],
        grid_spec=pltpu.PrefetchScalarGridSpec(
            num_scalar_prefetch=1,
            grid=(HALF // WCOLS,),
            in_specs=[quad] * (2 * places) + [columns, columns],
            out_specs=[pl.BlockSpec((SIDE, WCOLS // 128, SUB, 128), lambda n, s: (0, n, 0, 0))] * count,
            scratch_shapes=[pltpu.VMEM((count, 2, QUAD, TOK), BF)],
        ),
        compiler_params=pltpu.CompilerParams(vmem_limit_bytes=24 << 20),
        cost_estimate=pl.CostEstimate(
            flops=count * 4 * QUAD * TOK * HALF, transcendentals=0, bytes_accessed=4200000
        ),
        name="weight_quads",
    )(scalars, *owns, *others, grad_rows, grad_other)
    return [out.reshape(SIDE, PIECE, 128) for out in outs]


def order_kernel(s_ref, o_ref):
    segment, chip = s_ref[0], s_ref[1]
    x, y, z = chip & 3, (chip >> 2) & 3, chip >> 4
    p0 = (x + 2) & 3
    p1 = jnp.where(x == y, x + 1, y + 2) & 3
    p2 = (p0 + jnp.where(((p0 + 1) & 3) == p1, 2, 1)) & 3
    turn = jnp.where(segment == 0, x, y)
    sub = jnp.where(segment == 0, z, x)
    for n, value in enumerate((segment, turn, sub, x, y, z, p0, p1, p2, 6 - p0 - p1 - p2)):
        o_ref[n] = value


def order_scalars(where):
    smem = pl.BlockSpec(memory_space=pltpu.SMEM)
    return pl.pallas_call(
        order_kernel,
        out_shape=jax.ShapeDtypeStruct((ORDER + SIDE,), jnp.int32),
        in_specs=[smem],
        out_specs=smem,
        compiler_params=pltpu.CompilerParams(vmem_limit_bytes=1 << 20),
        cost_estimate=pl.CostEstimate(flops=6000000000, transcendentals=0, bytes_accessed=64),
        name="order",
    )(where)


def line_kernel(s_ref, own, r1, r2, r3, o0, o1, o2, o3):
    total = (own[0] + r2[0].astype(F32)) + (r1[0].astype(F32) + r3[0].astype(F32))
    for by, out in enumerate((o0, o1, o2, o3)):

        @pl.when(pl.program_id(0) == by)
        def _():
            out[...] = total.astype(out.dtype)


def sum_line(scalars, own, r1, r2, r3):
    block = pl.BlockSpec((1, PIECE, 128), lambda n, s: ((s[2] + n) % SIDE, 0, 0))
    whole = pl.BlockSpec((PIECE, 128), lambda n, s: (0, 0))
    return pl.pallas_call(
        line_kernel,
        out_shape=[jax.ShapeDtypeStruct((PIECE, 128), kind) for kind in (F32, BF, BF, BF)],
        grid_spec=pltpu.PrefetchScalarGridSpec(
            num_scalar_prefetch=1, grid=(SIDE,), in_specs=[block] * 4, out_specs=[whole] * 4
        ),
        compiler_params=pltpu.CompilerParams(vmem_limit_bytes=16 << 20),
        cost_estimate=pl.CostEstimate(flops=2000000, transcendentals=0, bytes_accessed=5000000),
        name="sum_line",
    )(scalars, own, r1, r2, r3)


def mid_kernel(own, r1, r2, r3, out):
    total = (own[...] + r2[...].astype(F32)) + (r1[...].astype(F32) + r3[...].astype(F32))
    out[...] = total.astype(BF)


def sum_mid(own, r1, r2, r3):
    return pl.pallas_call(
        mid_kernel,
        out_shape=jax.ShapeDtypeStruct((PIECE, 128), BF),
        compiler_params=pltpu.CompilerParams(vmem_limit_bytes=8 << 20),
        cost_estimate=pl.CostEstimate(flops=400000, transcendentals=0, bytes_accessed=1200000),
        name="sum_mid",
    )(own, r1, r2, r3)


def cross_kernel(own, r1, r2, r3, out):
    total = (own[...].astype(F32) + r2[...].astype(F32)) + (r1[...].astype(F32) + r3[...].astype(F32))
    out[:PIECE] = total.astype(BF)
    square = jnp.sum(total * total, 0, keepdims=True)
    terms = split_three(square)
    out[PIECE:] = jnp.concatenate(terms + (jnp.zeros((STAT - 3, 128), BF),), 0)


def sum_cross(own, r1, r2, r3):
    return pl.pallas_call(
        cross_kernel,
        out_shape=jax.ShapeDtypeStruct((PIECE + STAT, 128), BF),
        compiler_params=pltpu.CompilerParams(vmem_limit_bytes=8 << 20),
        cost_estimate=pl.CostEstimate(flops=600000, transcendentals=0, bytes_accessed=1200000),
        name="sum_cross",
    )(own, r1, r2, r3)


def split_three(x):
    high = x.astype(BF)
    rest = x - high.astype(F32)
    mid = rest.astype(BF)
    return high, mid, (rest - mid.astype(F32)).astype(BF)


def final_kernel(s_ref, *refs):
    pieces, later, out_hbm, dpk_hbm, dpv_hbm = refs[:8], refs[8], refs[9], refs[10], refs[11]
    bufs, outs, sem, out_sem = refs[12:]
    hand = [
        pltpu.make_async_copy(later.at[n], to, out_sem.at[8 + n]) for n, to in enumerate((dpk_hbm, dpv_hbm))
    ]
    for move in hand:
        move.start()
    segment, x, y, z = s_ref[0], s_ref[3], s_ref[4], s_ref[5]
    moves = [pltpu.make_async_copy(pieces[n], bufs.at[n], sem.at[n]) for n in range(8)]
    for move in moves:
        move.start()
    total = jnp.zeros((1, 128), F32)
    for n in range(8):
        moves[n].wait()
        for p in range(SIDE):
            stat = bufs[n, p, PIECE : PIECE + STAT, :].astype(F32)
            total = total + jnp.sum(stat, 0, keepdims=True)
    mean = jnp.sum(total, 1, keepdims=True) * (1.0 / (WIDTH * D))
    scale = jnp.minimum(1.0, 1.0 / jnp.sqrt(mean + 1e-06))
    writes = []
    for n in range(8):
        k = n % 4
        half = segment if n < 4 else 1 - segment
        quad = (jnp.where(half == 0, x, y) + SIDE - k) % SIDE
        at = jnp.where(half == 0, z, x)
        for p in range(SIDE):
            rows = pl.ds(pl.multiple_of((at + SIDE - p) % SIDE * SUB, 16), SUB)
            for tile in range(TILES):
                outs[n, rows, tile * 128 : tile * 128 + 128] = (
                    bufs[n, p, tile * SUB : tile * SUB + SUB, :].astype(F32) * scale
                ).astype(BF)
        write = pltpu.make_async_copy(
            outs.at[n],
            out_hbm.at[
                pl.ds(pl.multiple_of(quad * QUAD, 64), QUAD), pl.ds(pl.multiple_of(half * HALF, 128), HALF)
            ],
            out_sem.at[n],
        )
        write.start()
        writes.append(write)
    for write in writes + hand:
        write.wait()


def finish(scalars, pieces, later):
    any_spec = pl.BlockSpec(memory_space=pl.ANY)
    return pl.pallas_call(
        final_kernel,
        out_shape=(jax.ShapeDtypeStruct((WIDTH, D), BF),) + (jax.ShapeDtypeStruct((SUMS, WIDTH), BF),) * 2,
        grid_spec=pltpu.PrefetchScalarGridSpec(
            num_scalar_prefetch=1,
            grid=(1,),
            in_specs=[any_spec] * 9,
            out_specs=(any_spec,) * 3,
            scratch_shapes=[
                pltpu.VMEM((8, SIDE, PIECE + STAT, 128), BF),
                pltpu.VMEM((8, QUAD, HALF), BF),
                pltpu.SemaphoreType.DMA((8,)),
                pltpu.SemaphoreType.DMA((10,)),
            ],
        ),
        compiler_params=pltpu.CompilerParams(vmem_limit_bytes=32 << 20),
        cost_estimate=pl.CostEstimate(flops=7000000, transcendentals=0, bytes_accessed=14000000),
        name="clip",
    )(scalars, *pieces, later)


def hop(chip, axis, by):
    stride = {"x": 1, "y": SIDE, "z": SIDE * SIDE}[axis]
    at = (chip // stride) % SIDE
    return chip + (((at + by) % SIDE) - at) * stride


CHIPS = SIDE**3


def along(first, second, by):
    return [(c, hop(c, first, by)) for c in range(CHIPS)] + [
        (CHIPS + c, CHIPS + hop(c, second, by)) for c in range(CHIPS)
    ]


BOTH = ("seg", "dp")
SWAP = [(0, 1), (1, 0)]


def program(query_rows, key_rows, value_rows, prompt_keys, prompt_values, out_grad, w_out):
    q, k, v, grad_rows = query_rows[0], key_rows[0], value_rows[0], out_grad[0]
    grad_other = lax.ppermute(grad_rows, "seg", SWAP)
    where = jnp.stack([lax.axis_index("seg"), lax.axis_index("dp")]).astype(jnp.int32)
    scalars, prompt_keys, prompt_values = lax.optimization_barrier(
        (order_scalars(where), prompt_keys, prompt_values)
    )
    pk = lax.ppermute(prompt_keys[0], "seg", [(0, 1)])
    pv = lax.ppermute(prompt_values[0], "seg", [(0, 1)])

    attn, other, lses, sent = [], [], [], {}

    def forward(place, after=()):
        out, lse = forward_quad(place, scalars, q, k, v, pk, pv, after)
        attn.append(out)
        lses.append(lse)
        other.append(lax.ppermute(out, "seg", SWAP))

    def send(bys):
        parts = weight_quads(bys, scalars, attn, other, grad_rows, grad_other)
        for by, part in zip(bys, parts):
            sent[by] = lax.ppermute(part, BOTH, along("x", "y", by)) if by else part
        return parts

    forward(0)
    forward(1, (attn[0],))
    first = send((2,))
    forward(2, first)
    forward(3, first + [attn[2]])
    send((1, 3))
    send((0,))
    head_low = jnp.einsum("td,hd->th", grad_rows, w_out, preferred_element_type=F32).astype(BF)
    sent, head_low = lax.optimization_barrier((sent, head_low))
    own, *rest = sum_line(scalars, sent[0], sent[1], sent[2], sent[3])
    own = sum_mid(own, *[lax.ppermute(rest[by - 1], BOTH, along("z", "x", by)) for by in (1, 2, 3)])
    own = sum_cross(own, *[lax.ppermute(own, BOTH, along("y", "z", by)) for by in (1, 2, 3)])
    own = jnp.stack([own] + [lax.ppermute(own, BOTH, along("z", "x", by)) for by in (1, 2, 3)])

    own, head_low = lax.optimization_barrier((own, head_low))
    pieces = [own] + [lax.ppermute(own, BOTH, along("x", "y", by)) for by in (1, 2, 3)]
    dq, dk, dv, dp = backward(scalars, q, k, v, head_low, pk, pv, lses)
    pieces, dp = lax.optimization_barrier((pieces, dp))
    pieces = pieces + [lax.ppermute(part, "seg", SWAP) for part in pieces]
    weight_grad, dpk, dpv = finish(scalars, pieces, lax.ppermute(dp, "seg", [(1, 0)]))
    return (dq[None], dk[None], dv[None], dpk[None], dpv[None], weight_grad)


def solution(mesh):
    rows = P("dp", "seg", None)
    return jax.shard_map(
        program,
        mesh=mesh,
        in_specs=(rows,) * 6 + (P(),),
        out_specs=(rows,) * 5 + (P(),),
        check_vma=False,
    )
```

```python
import functools
import math

import jax
import jax.numpy as jnp
from jax import lax
from jax.experimental import pallas as pl
from jax.experimental.pallas import tpu as pltpu
from jax.sharding import PartitionSpec as P


HEADS = 16
HD = 80
SUMS = 50
PAD = 64
TOK = 512
WIDTH = HEADS * HD
D = 2560
HALF = D // 2
QUAD = 4 * HD
WIN = 384
BLK = 256
SCALE = HD**-0.5
C2 = SCALE * math.log2(math.e)
NEG = -1e30
SIDE = 4
TILES = HALF // 128
SUB = QUAD // SIDE
PIECE = SUB * TILES
STAT = 8
ORDER = 6
BF = jnp.bfloat16
F32 = jnp.float32


def dot(a, b):
    return lax.dot_general(a, b, (((1,), (0,)), ((), ())), preferred_element_type=F32)


def dot_nt(a, b):
    return lax.dot_general(a, b, (((1,), (1,)), ((), ())), preferred_element_type=F32)


def iota(shape, dim):
    return lax.broadcasted_iota(jnp.int32, shape, dim)


def fwd_kernel(place, s_ref, q_ref, k_ref, v_ref, prompt_ref, *rest):
    o_ref, lse_ref, pk_ref, vt_ref, pvt_ref = rest[-5:]
    segment, quad = s_ref[0], s_ref[ORDER + place]
    odd = quad & 1
    start = ((quad * 5) >> 1) * 128
    window = pl.ds(pl.multiple_of(start, 128), WIN)
    rows = jnp.zeros((PAD - SUMS, WIN), BF)
    pk_ref[...] = jnp.concatenate([prompt_ref[0, :, window], rows], 0)
    vt_ref[...] = jnp.transpose(v_ref[:, window])
    pvt_ref[...] = jnp.transpose(jnp.concatenate([prompt_ref[1, :, window], rows], 0))
    lanes = iota((TOK, BLK), 1)
    causal = iota((BLK, BLK), 0) <= iota((BLK, BLK), 1)
    seen = iota((PAD, TOK), 0) < SUMS * segment

    def head(h, at):
        low = 64 * odd + HD * h - at
        w = pl.ds(pl.multiple_of(start + at, 128), BLK)
        mine = (lanes >= low) & (lanes < low + HD)
        qm = jnp.where(mine, q_ref[:, w], jnp.zeros((), BF))
        s0 = dot_nt(k_ref[:BLK, w], qm)
        s1 = dot_nt(k_ref[BLK:, w], qm[BLK:])
        sp = jnp.where(seen, dot_nt(pk_ref[:, at : at + BLK], qm), NEG)
        s00 = jnp.where(causal, s0[:, :BLK], NEG)
        s01 = s0[:, BLK:]
        s11 = jnp.where(causal, s1, NEG)
        mp = jnp.max(sp, 0, keepdims=True)
        m0 = jnp.maximum(jnp.max(s00, 0, keepdims=True), mp[:, :BLK])
        m1 = jnp.maximum(
            jnp.maximum(jnp.max(s01, 0, keepdims=True), jnp.max(s11, 0, keepdims=True)), mp[:, BLK:]
        )
        e00 = jnp.exp2((s00 - m0) * C2)
        e01 = jnp.exp2((s01 - m1) * C2)
        e11 = jnp.exp2((s11 - m1) * C2)
        ep0 = jnp.exp2((sp[:, :BLK] - m0) * C2)
        ep1 = jnp.exp2((sp[:, BLK:] - m1) * C2)
        l0 = jnp.sum(e00, 0, keepdims=True) + jnp.sum(ep0, 0, keepdims=True)
        l1 = (
            jnp.sum(e01, 0, keepdims=True)
            + jnp.sum(e11, 0, keepdims=True)
            + jnp.sum(ep1, 0, keepdims=True)
        )
        row = pl.ds(pl.multiple_of(64 * odd + HD * h, 16), HD)
        to = slice(HD * h, HD * h + HD)
        vt = vt_ref[row, :]
        pvt = pvt_ref[row, :]
        o0 = dot(vt[:, :BLK], e00.astype(BF)) + dot(pvt, ep0.astype(BF))
        o1 = (
            dot(vt[:, :BLK], e01.astype(BF))
            + dot(vt[:, BLK:], e11.astype(BF))
            + dot(pvt, ep1.astype(BF))
        )
        o_ref[to, :BLK] = (o0 / l0).astype(BF)
        o_ref[to, BLK:] = (o1 / l1).astype(BF)
        lse_ref[pl.ds(h, 1), :BLK] = m0 * C2 + jnp.log2(l0)
        lse_ref[pl.ds(h, 1), BLK:] = m1 * C2 + jnp.log2(l1)

    for h in range(4):
        head(h, h // 2 * 128)


def forward_quad(place, scalars, q, k, v, prompts, after):
    vmem = pl.BlockSpec(memory_space=pltpu.VMEM)
    return pl.pallas_call(
        functools.partial(fwd_kernel, place),
        out_shape=(jax.ShapeDtypeStruct((QUAD, TOK), BF), jax.ShapeDtypeStruct((4, TOK), F32)),
        in_specs=[pl.BlockSpec(memory_space=pltpu.SMEM)]
        + [vmem] * 4
        + [pl.BlockSpec(memory_space=pl.ANY)] * len(after),
        out_specs=(vmem, vmem),
        scratch_shapes=[
            pltpu.VMEM((PAD, WIN), BF),
            pltpu.VMEM((WIN, TOK), BF),
            pltpu.VMEM((WIN, PAD), BF),
        ],
        compiler_params=pltpu.CompilerParams(vmem_limit_bytes=24 << 20),
        cost_estimate=pl.CostEstimate(
            flops=4 * 2 * 2 * 896 * 256 * 256, transcendentals=4 * 896 * 256, bytes_accessed=1600000
        ),
        name="fwd_quad",
    )(scalars, q, k, v, prompts, *after)


def bwd_kernel(
    s_ref, q_ref, k_ref, v_ref, g_ref, prompt_ref, lse_0, lse_1, lse_2, lse_3,
    dq_ref, dk_ref, dv_ref, dp_ref,
    kt_ref, pkt_ref, dqt_ref, dka_ref, dva_ref, dpka_ref, dpva_ref, pk_ref, pv_ref, lse_ref,
):
    for n in range(2):
        lse = lse_0[...]
        for place, other in ((1, lse_1), (2, lse_2), (3, lse_3)):
            lse = jnp.where(s_ref[ORDER + place] == 2 * pl.program_id(0) + n, other[...], lse)
        lse_ref[4 * n : 4 * n + 4] = lse
    segment = s_ref[0]
    pk_ref[...] = jnp.zeros_like(pk_ref)
    pv_ref[...] = jnp.zeros_like(pv_ref)
    pk_ref[:SUMS] = prompt_ref[0]
    pv_ref[:SUMS] = prompt_ref[1]
    kt_ref[...] = jnp.transpose(k_ref[...])
    pkt_ref[...] = jnp.transpose(pk_ref[...])
    for acc in (dka_ref, dva_ref, dpka_ref, dpva_ref):
        acc[...] = jnp.zeros_like(acc)
    causal = iota((BLK, BLK), 0) <= iota((BLK, BLK), 1)
    seen = iota((PAD, TOK), 0) < SUMS * segment
    for h in range(8):
        low = HD * h
        at = low // 128 * 128
        wide = 128 if low - at + HD <= 128 else 256
        w = slice(at, at + wide)
        lanes = iota((TOK, wide), 1) + at
        mine = (lanes >= low) & (lanes < low + HD)
        qm = jnp.where(mine, q_ref[:, w], jnp.zeros((), BF))
        gm = jnp.where(mine, g_ref[:, w], jnp.zeros((), BF))
        lse = lse_ref[h : h + 1, :]
        lse0, lse1 = lse[:, :BLK], lse[:, BLK:]
        s0 = dot_nt(k_ref[:BLK, w], qm)
        s1 = dot_nt(k_ref[BLK:, w], qm[BLK:])
        sp = dot_nt(pk_ref[:, w], qm)
        p00 = jnp.exp2(jnp.where(causal, s0[:, :BLK] * C2 - lse0, NEG))
        p01 = jnp.exp2(s0[:, BLK:] * C2 - lse1)
        p11 = jnp.exp2(jnp.where(causal, s1 * C2 - lse1, NEG))
        pp = jnp.exp2(jnp.where(seen, sp * C2 - lse, NEG))
        d0 = dot_nt(v_ref[:BLK, w], gm)
        d11 = dot_nt(v_ref[BLK:, w], gm[BLK:])
        dp = dot_nt(pv_ref[:, w], gm)
        d00, d01 = d0[:, :BLK], d0[:, BLK:]
        deltap = jnp.sum(pp * dp, 0, keepdims=True)
        delta0 = jnp.sum(p00 * d00, 0, keepdims=True) + deltap[:, :BLK]
        delta1 = (
            jnp.sum(p01 * d01, 0, keepdims=True)
            + jnp.sum(p11 * d11, 0, keepdims=True)
            + deltap[:, BLK:]
        )
        delta = jnp.concatenate([delta0, delta1], 1)
        t00 = (p00 * (d00 - delta0) * SCALE).astype(BF)
        t01 = (p01 * (d01 - delta1) * SCALE).astype(BF)
        t11 = (p11 * (d11 - delta1) * SCALE).astype(BF)
        tp = (pp * (dp - delta) * SCALE).astype(BF)
        t0 = jnp.concatenate([t00, t01], 1)
        row = slice(low, low + HD)
        dqt = dot(kt_ref[row, :BLK], t0) + dot(pkt_ref[row, :], tp)
        dqt_ref[row, :BLK] = dqt[:, :BLK].astype(BF)
        dqt_ref[row, BLK:] = (dqt[:, BLK:] + dot(kt_ref[row, BLK:], t11)).astype(BF)
        dka_ref[:BLK, w] += dot(t0, qm)
        dka_ref[BLK:, w] += dot(t11, qm[BLK:])
        dpka_ref[:, w] += dot(tp, qm)
        low0 = jnp.concatenate([p00.astype(BF), p01.astype(BF)], 1)
        dva_ref[:BLK, w] += dot(low0, gm)
        dva_ref[BLK:, w] += dot(p11.astype(BF), gm[BLK:])
        dpva_ref[:, w] += dot(pp.astype(BF), gm)
    dq_ref[...] = jnp.transpose(dqt_ref[...])
    dk_ref[...] = dka_ref[...].astype(BF)
    dv_ref[...] = dva_ref[...].astype(BF)
    dp_ref[0] = dpka_ref[:SUMS].astype(BF)
    dp_ref[1] = dpva_ref[:SUMS].astype(BF)


def backward(scalars, q, k, v, g, prompts, lses):
    wide = 8 * HD
    rows = pl.BlockSpec((TOK, wide), lambda i, s: (0, i))
    prompt = pl.BlockSpec((2, SUMS, wide), lambda i, s: (0, 0, i))
    return pl.pallas_call(
        bwd_kernel,
        out_shape=(jax.ShapeDtypeStruct((TOK, WIDTH), BF),) * 3
        + (jax.ShapeDtypeStruct((2, SUMS, WIDTH), BF),),
        grid_spec=pltpu.PrefetchScalarGridSpec(
            num_scalar_prefetch=1,
            grid=(2,),
            in_specs=[rows] * 4 + [prompt] + [pl.BlockSpec((4, TOK), lambda i, s: (0, 0))] * 4,
            out_specs=(rows, rows, rows, prompt),
            scratch_shapes=[
                pltpu.VMEM((wide, TOK), BF),
                pltpu.VMEM((wide, PAD), BF),
                pltpu.VMEM((wide, TOK), BF),
                pltpu.VMEM((TOK, wide), F32),
                pltpu.VMEM((TOK, wide), F32),
                pltpu.VMEM((PAD, wide), F32),
                pltpu.VMEM((PAD, wide), F32),
                pltpu.VMEM((PAD, wide), BF),
                pltpu.VMEM((PAD, wide), BF),
                pltpu.VMEM((8, TOK), F32),
            ],
        ),
        compiler_params=pltpu.CompilerParams(vmem_limit_bytes=36 << 20),
        cost_estimate=pl.CostEstimate(
            flops=16 * 5 * 2 * 896 * 256 * 256, transcendentals=16 * 896 * 256, bytes_accessed=10000000
        ),
        name="attend_back",
    )(scalars, q, k, v, g, prompts, *lses)


WCOLS = 640


def weight_kernel(bys, places, s_ref, *refs):
    owns, others, g_ref, h_ref = refs[:places], refs[places : 2 * places], refs[2 * places], refs[2 * places + 1]
    outs, picked = refs[2 * places + 2 : -1], refs[-1]
    for n, by in enumerate(bys):
        quad = (s_ref[1] + by) & (SIDE - 1)
        for j in range(places):

            @pl.when(quad == s_ref[ORDER + j])
            def _():
                picked[n, 0] = owns[j][...]
                picked[n, 1] = others[j][...]

    for n, out_ref in enumerate(outs):
        for part in range(HALF // WCOLS):
            w = pl.ds(pl.multiple_of(s_ref[0] * HALF + part * WCOLS, 128), WCOLS)
            out = dot(picked[n, 0], g_ref[:, w]) + dot(picked[n, 1], h_ref[:, w])
            for sub in range(SIDE):
                for tile in range(WCOLS // 128):
                    out_ref[sub, part * (WCOLS // 128) + tile] = out[
                        sub * SUB : sub * SUB + SUB, tile * 128 : tile * 128 + 128
                    ].astype(out_ref.dtype)


def weight_quads(bys, scalars, owns, others, grad_rows, grad_other):
    count, places = len(bys), len(owns)
    vmem = pl.BlockSpec(memory_space=pltpu.VMEM)
    outs = pl.pallas_call(
        functools.partial(weight_kernel, bys, places),
        out_shape=[jax.ShapeDtypeStruct((SIDE, TILES, SUB, 128), BF if by else F32) for by in bys],
        in_specs=[pl.BlockSpec(memory_space=pltpu.SMEM)] + [vmem] * (2 * places + 2),
        out_specs=[vmem] * count,
        scratch_shapes=[pltpu.VMEM((count, 2, QUAD, TOK), BF)],
        compiler_params=pltpu.CompilerParams(vmem_limit_bytes=16 << 20),
        cost_estimate=pl.CostEstimate(
            flops=count * 4 * QUAD * TOK * HALF, transcendentals=0, bytes_accessed=4200000
        ),
        name="weight_quads",
    )(scalars, *owns, *others, grad_rows, grad_other)
    return [out.reshape(SIDE, PIECE, 128) for out in outs]


def line_kernel(s_ref, own, r1, r2, r3, *outs):
    for by, out in enumerate(outs):
        n = (s_ref[2] + by) & (SIDE - 1)
        total = (own[n] + r2[n].astype(F32)) + (r1[n].astype(F32) + r3[n].astype(F32))
        out[...] = total.astype(out.dtype)


def sum_line(scalars, own, r1, r2, r3):
    vmem = pl.BlockSpec(memory_space=pltpu.VMEM)
    return pl.pallas_call(
        line_kernel,
        out_shape=[jax.ShapeDtypeStruct((PIECE, 128), kind) for kind in (F32, BF, BF, BF)],
        in_specs=[pl.BlockSpec(memory_space=pltpu.SMEM)] + [vmem] * 4,
        out_specs=[vmem] * 4,
        compiler_params=pltpu.CompilerParams(vmem_limit_bytes=8 << 20),
        cost_estimate=pl.CostEstimate(flops=2000000, transcendentals=0, bytes_accessed=5000000),
        name="sum_line",
    )(scalars, own, r1, r2, r3)


def order_kernel(s_ref, o_ref):
    segment, chip = s_ref[0], s_ref[1]
    x, y, z = chip & 3, (chip >> 2) & 3, chip >> 4
    p0 = (x + 2) & 3
    p1 = jnp.where(x == y, x + 1, y + 2) & 3
    p2 = (p0 + jnp.where(((p0 + 1) & 3) == p1, 2, 1)) & 3
    turn = jnp.where(segment == 0, x, y)
    sub = jnp.where(segment == 0, z, x)
    for n, value in enumerate((segment, turn, sub, x, y, z, p0, p1, p2, 6 - p0 - p1 - p2)):
        o_ref[n] = value


def order_scalars(where):
    smem = pl.BlockSpec(memory_space=pltpu.SMEM)
    return pl.pallas_call(
        order_kernel,
        out_shape=jax.ShapeDtypeStruct((ORDER + SIDE,), jnp.int32),
        in_specs=[smem],
        out_specs=smem,
        compiler_params=pltpu.CompilerParams(vmem_limit_bytes=1 << 20),
        cost_estimate=pl.CostEstimate(flops=6000000000, transcendentals=0, bytes_accessed=64),
        name="order",
    )(where)


def mid_kernel(own, r1, r2, r3, out):
    total = (own[...] + r2[...].astype(F32)) + (r1[...].astype(F32) + r3[...].astype(F32))
    out[...] = total.astype(BF)


def sum_mid(own, r1, r2, r3):
    return pl.pallas_call(
        mid_kernel,
        out_shape=jax.ShapeDtypeStruct((PIECE, 128), BF),
        compiler_params=pltpu.CompilerParams(vmem_limit_bytes=8 << 20),
        cost_estimate=pl.CostEstimate(flops=400000, transcendentals=0, bytes_accessed=1200000),
        name="sum_mid",
    )(own, r1, r2, r3)


def cross_kernel(own, r1, r2, r3, out):
    total = (own[...].astype(F32) + r2[...].astype(F32)) + (r1[...].astype(F32) + r3[...].astype(F32))
    out[:PIECE] = total.astype(BF)
    square = jnp.sum(total * total, 0, keepdims=True)
    terms = split_three(square)
    out[PIECE:] = jnp.concatenate(terms + (jnp.zeros((STAT - 3, 128), BF),), 0)


def sum_cross(own, r1, r2, r3):
    return pl.pallas_call(
        cross_kernel,
        out_shape=jax.ShapeDtypeStruct((PIECE + STAT, 128), BF),
        compiler_params=pltpu.CompilerParams(vmem_limit_bytes=8 << 20),
        cost_estimate=pl.CostEstimate(flops=600000, transcendentals=0, bytes_accessed=1200000),
        name="sum_cross",
    )(own, r1, r2, r3)


def split_three(x):
    high = x.astype(BF)
    rest = x - high.astype(F32)
    mid = rest.astype(BF)
    return high, mid, (rest - mid.astype(F32)).astype(BF)


def final_kernel(s_ref, *refs):
    pieces, later, out_hbm, dpk_hbm, dpv_hbm = refs[:8], refs[8], refs[9], refs[10], refs[11]
    outs, out_sem = refs[12:]
    hand = [
        pltpu.make_async_copy(later.at[n], to, out_sem.at[8 + n]) for n, to in enumerate((dpk_hbm, dpv_hbm))
    ]
    for move in hand:
        move.start()
    segment, x, y, z = s_ref[0], s_ref[3], s_ref[4], s_ref[5]
    total = jnp.zeros((1, 128), F32)
    for piece in pieces:
        for p in range(SIDE):
            total = total + jnp.sum(piece[p, PIECE : PIECE + STAT, :].astype(F32), 0, keepdims=True)
    mean = jnp.sum(total, 1, keepdims=True) * (1.0 / (WIDTH * D))
    scale = jnp.minimum(1.0, 1.0 / jnp.sqrt(mean + 1e-06))
    writes = []
    for n in range(8):
        k = n % 4
        half = segment if n < 4 else 1 - segment
        quad = (jnp.where(half == 0, x, y) + SIDE - k) % SIDE
        at = jnp.where(half == 0, z, x)
        for p in range(SIDE):
            rows = pl.ds(pl.multiple_of((at + SIDE - p) % SIDE * SUB, 16), SUB)
            for tile in range(TILES):
                outs[n, rows, tile * 128 : tile * 128 + 128] = (
                    pieces[n][p, tile * SUB : tile * SUB + SUB, :].astype(F32) * scale
                ).astype(BF)
        write = pltpu.make_async_copy(
            outs.at[n],
            out_hbm.at[
                pl.ds(pl.multiple_of(quad * QUAD, 64), QUAD), pl.ds(pl.multiple_of(half * HALF, 128), HALF)
            ],
            out_sem.at[n],
        )
        write.start()
        writes.append(write)
    for write in writes + hand:
        write.wait()


def finish(scalars, pieces, later):
    vmem, any_spec = pl.BlockSpec(memory_space=pltpu.VMEM), pl.BlockSpec(memory_space=pl.ANY)
    return pl.pallas_call(
        final_kernel,
        out_shape=(jax.ShapeDtypeStruct((WIDTH, D), BF),) + (jax.ShapeDtypeStruct((SUMS, WIDTH), BF),) * 2,
        in_specs=[pl.BlockSpec(memory_space=pltpu.SMEM)] + [vmem] * 8 + [any_spec],
        out_specs=(any_spec,) * 3,
        scratch_shapes=[
            pltpu.VMEM((8, QUAD, HALF), BF),
            pltpu.SemaphoreType.DMA((10,)),
        ],
        compiler_params=pltpu.CompilerParams(vmem_limit_bytes=16 << 20),
        cost_estimate=pl.CostEstimate(flops=7000000, transcendentals=0, bytes_accessed=14000000),
        name="clip",
    )(scalars, *pieces, later)


def hop(chip, axis, by):
    stride = {"x": 1, "y": SIDE, "z": SIDE * SIDE}[axis]
    at = (chip // stride) % SIDE
    return chip + (((at + by) % SIDE) - at) * stride


CHIPS = SIDE**3


def along(first, second, by):
    return [(c, hop(c, first, by)) for c in range(CHIPS)] + [
        (CHIPS + c, CHIPS + hop(c, second, by)) for c in range(CHIPS)
    ]


BOTH = ("seg", "dp")
SWAP = [(0, 1), (1, 0)]


def program(query_rows, key_rows, value_rows, prompt_keys, prompt_values, out_grad, w_out):
    q, k, v, grad_rows = query_rows[0], key_rows[0], value_rows[0], out_grad[0]
    grad_other = lax.ppermute(grad_rows, "seg", SWAP)
    where = jnp.stack([lax.axis_index("seg"), lax.axis_index("dp")]).astype(jnp.int32)
    scalars, prompts = lax.optimization_barrier(
        (order_scalars(where), jnp.stack([prompt_keys[0], prompt_values[0]]))
    )
    prompts = lax.ppermute(prompts, "seg", [(0, 1)])

    attn, other, lses, sent = [], [], [], {}

    def forward(place, after=()):
        out, lse = forward_quad(place, scalars, q, k, v, prompts, after)
        attn.append(out)
        lses.append(lse)
        other.append(lax.ppermute(out, "seg", SWAP))

    def send(bys):
        parts = weight_quads(bys, scalars, attn, other, grad_rows, grad_other)
        for by, part in zip(bys, parts):
            sent[by] = lax.ppermute(part, BOTH, along("x", "y", by)) if by else part
        return parts

    forward(0)
    forward(1, (attn[0],))
    first = send((2,))
    forward(2, first)
    forward(3, first + [attn[2]])
    send((1, 3))
    send((0,))
    head_low = jnp.einsum("td,hd->th", grad_rows, w_out, preferred_element_type=F32).astype(BF)
    sent, head_low = lax.optimization_barrier((sent, head_low))
    own, *rest = sum_line(scalars, sent[0], sent[1], sent[2], sent[3])
    own = sum_mid(own, *[lax.ppermute(rest[by - 1], BOTH, along("z", "x", by)) for by in (1, 2, 3)])
    own = sum_cross(own, *[lax.ppermute(own, BOTH, along("y", "z", by)) for by in (1, 2, 3)])
    own = jnp.stack([own] + [lax.ppermute(own, BOTH, along("z", "x", by)) for by in (1, 2, 3)])

    own, head_low = lax.optimization_barrier((own, head_low))
    pieces = [lax.ppermute(own, BOTH, along("x", "y", by)) for by in (1, 2, 3)]
    dq, dk, dv, dp = backward(scalars, q, k, v, head_low, prompts, lses)
    own, dp = lax.optimization_barrier((own, dp))
    later = lax.ppermute(dp, "seg", [(1, 0)])
    swapped = [lax.ppermute(own, "seg", SWAP)]
    for n in range(3):
        pieces[n], _ = lax.optimization_barrier((pieces[n], dp))
        swapped.append(lax.ppermute(pieces[n], "seg", SWAP))
    weight_grad, dpk, dpv = finish(scalars, [own] + pieces + swapped, later)
    return (dq[None], dk[None], dv[None], dpk[None], dpv[None], weight_grad)


def solution(mesh):
    rows = P("dp", "seg", None)
    return jax.shard_map(
        program,
        mesh=mesh,
        in_specs=(rows,) * 6 + (P(),),
        out_specs=(rows,) * 5 + (P(),),
        check_vma=False,
    )
```

```python
import functools
import math

import jax
import jax.numpy as jnp
from jax import lax
from jax.experimental import pallas as pl
from jax.experimental.pallas import tpu as pltpu
from jax.sharding import PartitionSpec as P


HEADS = 16
HD = 80
SUMS = 50
PAD = 64
TOK = 512
WIDTH = HEADS * HD
D = 2560
HALF = D // 2
QUAD = 4 * HD
WIN = 384
BLK = 256
SCALE = HD**-0.5
C2 = SCALE * math.log2(math.e)
NEG = -1e30
SIDE = 4
TILES = HALF // 128
SUB = QUAD // SIDE
PIECE = SUB * TILES
STAT = 8
ORDER = 6
BF = jnp.bfloat16
F32 = jnp.float32


def dot(a, b):
    return lax.dot_general(a, b, (((1,), (0,)), ((), ())), preferred_element_type=F32)


def dot_nt(a, b):
    return lax.dot_general(a, b, (((1,), (1,)), ((), ())), preferred_element_type=F32)


def iota(shape, dim):
    return lax.broadcasted_iota(jnp.int32, shape, dim)


def fwd_kernel(places, s_ref, q_ref, k_ref, v_ref, prompt_ref, *rest):
    out_ref, lses, (pk_ref, vt_ref, pvt_ref) = rest[-6], rest[-5:-3], rest[-3:]
    segment = s_ref[0]
    causal = iota((BLK, BLK), 0) <= iota((BLK, BLK), 1)
    seen = iota((PAD, TOK), 0) < SUMS * segment
    lanes = iota((TOK, BLK), 1)
    odds, starts = [], []
    for n, place in enumerate(places):
        quad = s_ref[ORDER + place]
        odds.append(quad & 1)
        starts.append(((quad * 5) >> 1) * 128)
        window = pl.ds(pl.multiple_of(starts[n], 128), WIN)
        rows = jnp.zeros((PAD - SUMS, WIN), BF)
        pk_ref[n] = jnp.concatenate([prompt_ref[0, :, window], rows], 0)
        vt_ref[n] = jnp.transpose(v_ref[:, window])
        pvt_ref[n] = jnp.transpose(jnp.concatenate([prompt_ref[1, :, window], rows], 0))

    def score(n, h):
        at = h // 2 * 128
        low = 64 * odds[n] + HD * h - at
        w = pl.ds(pl.multiple_of(starts[n] + at, 128), BLK)
        mine = (lanes >= low) & (lanes < low + HD)
        qm = jnp.where(mine, q_ref[:, w], jnp.zeros((), BF))
        s0 = dot_nt(k_ref[:BLK, w], qm)
        s1 = dot_nt(k_ref[BLK:, w], qm[BLK:])
        sp = dot_nt(pk_ref[n, :, at : at + BLK], qm)
        return s0, s1, sp

    def soften(n, h, s0, s1, sp):
        sp = jnp.where(seen, sp, NEG)
        s00 = jnp.where(causal, s0[:, :BLK], NEG)
        s01 = s0[:, BLK:]
        s11 = jnp.where(causal, s1, NEG)
        mp = jnp.max(sp, 0, keepdims=True)
        m0 = jnp.maximum(jnp.max(s00, 0, keepdims=True), mp[:, :BLK])
        m1 = jnp.maximum(
            jnp.maximum(jnp.max(s01, 0, keepdims=True), jnp.max(s11, 0, keepdims=True)), mp[:, BLK:]
        )
        e00 = jnp.exp2((s00 - m0) * C2)
        e01 = jnp.exp2((s01 - m1) * C2)
        e11 = jnp.exp2((s11 - m1) * C2)
        ep0 = jnp.exp2((sp[:, :BLK] - m0) * C2)
        ep1 = jnp.exp2((sp[:, BLK:] - m1) * C2)
        l0 = jnp.sum(e00, 0, keepdims=True) + jnp.sum(ep0, 0, keepdims=True)
        l1 = (
            jnp.sum(e01, 0, keepdims=True)
            + jnp.sum(e11, 0, keepdims=True)
            + jnp.sum(ep1, 0, keepdims=True)
        )
        lses[n][h : h + 1, :BLK] = m0 * C2 + jnp.log2(l0)
        lses[n][h : h + 1, BLK:] = m1 * C2 + jnp.log2(l1)
        return tuple(e.astype(BF) for e in (e00, e01, e11, ep0, ep1)) + (l0, l1)

    def attend(n, h, e00, e01, e11, ep0, ep1, l0, l1):
        row = pl.ds(pl.multiple_of(64 * odds[n] + HD * h, 16), HD)
        to = slice(HD * h, HD * h + HD)
        vt = vt_ref[n, row, :]
        pvt = pvt_ref[n, row, :]
        o0 = dot(vt[:, :BLK], e00) + dot(pvt, ep0)
        o1 = dot(vt[:, :BLK], e01) + dot(vt[:, BLK:], e11) + dot(pvt, ep1)
        out_ref[n, to, :BLK] = (o0 / l0).astype(BF)
        out_ref[n, to, BLK:] = (o1 / l1).astype(BF)

    heads = [(n, h) for n in range(len(places)) for h in range(4)]
    scores, weights = {0: score(*heads[0])}, {}
    for i in range(len(heads) + 1):
        if i + 1 < len(heads):
            scores[i + 1] = score(*heads[i + 1])
        if i > 0:
            attend(*heads[i - 1], *weights.pop(i - 1))
        if i < len(heads):
            weights[i] = soften(*heads[i], *scores.pop(i))


def forward_quads(places, scalars, q, k, v, prompts, after):
    vmem = pl.BlockSpec(memory_space=pltpu.VMEM)
    count = len(places)
    outs = pl.pallas_call(
        functools.partial(fwd_kernel, places),
        out_shape=[jax.ShapeDtypeStruct((count, QUAD, TOK), BF)]
        + [jax.ShapeDtypeStruct((4, TOK), F32)] * count,
        in_specs=[pl.BlockSpec(memory_space=pltpu.SMEM)]
        + [vmem] * 4
        + [pl.BlockSpec(memory_space=pl.ANY)] * len(after),
        out_specs=[vmem] * (1 + count),
        scratch_shapes=[
            pltpu.VMEM((count, PAD, WIN), BF),
            pltpu.VMEM((count, WIN, TOK), BF),
            pltpu.VMEM((count, WIN, PAD), BF),
        ],
        compiler_params=pltpu.CompilerParams(vmem_limit_bytes=24 << 20),
        cost_estimate=pl.CostEstimate(
            flops=8 * 2 * 2 * 896 * 256 * 256, transcendentals=8 * 896 * 256, bytes_accessed=3200000
        ),
        name="fwd_quads",
    )(scalars, q, k, v, prompts, *after)
    return outs[0], outs[1:]


def bwd_kernel(
    s_ref, q_ref, k_ref, v_ref, g_ref, prompt_ref, lse_0, lse_1, lse_2, lse_3,
    dq_ref, dk_ref, dv_ref, dp_ref,
    kt_ref, pkt_ref, dqt_ref, dka_ref, dva_ref, dpka_ref, dpva_ref, pk_ref, pv_ref, lse_ref,
):
    base = pl.program_id(0) * 8 * HD
    whole = pl.ds(pl.multiple_of(base, 128), 8 * HD)
    for n in range(2):
        lse = lse_0[...]
        for place, other in ((1, lse_1), (2, lse_2), (3, lse_3)):
            lse = jnp.where(s_ref[ORDER + place] == 2 * pl.program_id(0) + n, other[...], lse)
        lse_ref[4 * n : 4 * n + 4] = lse
    segment = s_ref[0]
    pk_ref[...] = jnp.zeros_like(pk_ref)
    pv_ref[...] = jnp.zeros_like(pv_ref)
    pk_ref[:SUMS] = prompt_ref[0]
    pv_ref[:SUMS] = prompt_ref[1]
    kt_ref[...] = jnp.transpose(k_ref[:, whole])
    pkt_ref[...] = jnp.transpose(pk_ref[...])
    for acc in (dka_ref, dva_ref, dpka_ref, dpva_ref):
        acc[...] = jnp.zeros_like(acc)
    causal = iota((BLK, BLK), 0) <= iota((BLK, BLK), 1)
    seen = iota((PAD, TOK), 0) < SUMS * segment

    def place(h):
        low = HD * h
        at = low // 128 * 128
        wide = 128 if low - at + HD <= 128 else 256
        return slice(low, low + HD), slice(at, at + wide), low - at, wide

    def columns(h):
        _, w, _, wide = place(h)
        return pl.ds(pl.multiple_of(base + w.start, 128), wide)

    def masked(h, ref):
        _, _, low, wide = place(h)
        lanes = iota((TOK, wide), 1)
        return jnp.where((lanes >= low) & (lanes < low + HD), ref[:, columns(h)], jnp.zeros((), BF))

    def score(h):
        w, c = place(h)[1], columns(h)
        qm, gm = masked(h, q_ref), masked(h, g_ref)
        return (
            dot_nt(k_ref[:BLK, c], qm),
            dot_nt(k_ref[BLK:, c], qm[BLK:]),
            dot_nt(pk_ref[:, w], qm),
            dot_nt(v_ref[:BLK, c], gm),
            dot_nt(v_ref[BLK:, c], gm[BLK:]),
            dot_nt(pv_ref[:, w], gm),
        )

    def soften(h, s0, s1, sp, d0, d11, dp):
        lse = lse_ref[h : h + 1, :]
        lse0, lse1 = lse[:, :BLK], lse[:, BLK:]
        p00 = jnp.exp2(jnp.where(causal, s0[:, :BLK] * C2 - lse0, NEG))
        p01 = jnp.exp2(s0[:, BLK:] * C2 - lse1)
        p11 = jnp.exp2(jnp.where(causal, s1 * C2 - lse1, NEG))
        pp = jnp.exp2(jnp.where(seen, sp * C2 - lse, NEG))
        d00, d01 = d0[:, :BLK], d0[:, BLK:]
        deltap = jnp.sum(pp * dp, 0, keepdims=True)
        delta0 = jnp.sum(p00 * d00, 0, keepdims=True) + deltap[:, :BLK]
        delta1 = (
            jnp.sum(p01 * d01, 0, keepdims=True)
            + jnp.sum(p11 * d11, 0, keepdims=True)
            + deltap[:, BLK:]
        )
        delta = jnp.concatenate([delta0, delta1], 1)
        t00 = (p00 * (d00 - delta0) * SCALE).astype(BF)
        t01 = (p01 * (d01 - delta1) * SCALE).astype(BF)
        t11 = (p11 * (d11 - delta1) * SCALE).astype(BF)
        tp = (pp * (dp - delta) * SCALE).astype(BF)
        t0 = jnp.concatenate([t00, t01], 1)
        low0 = jnp.concatenate([p00.astype(BF), p01.astype(BF)], 1)
        return t0, t11, tp, low0, p11.astype(BF), pp.astype(BF)

    def spread(h, t0, t11, tp, low0, low11, lowp):
        row, w = place(h)[:2]
        qm, gm = masked(h, q_ref), masked(h, g_ref)
        dqt = dot(kt_ref[row, :BLK], t0) + dot(pkt_ref[row, :], tp)
        dqt_ref[row, :BLK] = dqt[:, :BLK].astype(BF)
        dqt_ref[row, BLK:] = (dqt[:, BLK:] + dot(kt_ref[row, BLK:], t11)).astype(BF)
        dka_ref[:BLK, w] += dot(t0, qm)
        dka_ref[BLK:, w] += dot(t11, qm[BLK:])
        dpka_ref[:, w] += dot(tp, qm)
        dva_ref[:BLK, w] += dot(low0, gm)
        dva_ref[BLK:, w] += dot(low11, gm[BLK:])
        dpva_ref[:, w] += dot(lowp, gm)

    scores, weights = {0: score(0)}, {}
    for h in range(9):
        if h > 0:
            spread(h - 1, *weights.pop(h - 1))
        if h < 7:
            scores[h + 1] = score(h + 1)
        if h < 8:
            weights[h] = soften(h, *scores.pop(h))
    dq_ref[...] = jnp.transpose(dqt_ref[...])
    dk_ref[...] = dka_ref[...].astype(BF)
    dv_ref[...] = dva_ref[...].astype(BF)
    dp_ref[0] = dpka_ref[:SUMS].astype(BF)
    dp_ref[1] = dpva_ref[:SUMS].astype(BF)


def backward(scalars, q, k, v, g, prompts, lses):
    wide = 8 * HD
    rows = pl.BlockSpec((TOK, wide), lambda i, s: (0, i))
    prompt = pl.BlockSpec((2, SUMS, wide), lambda i, s: (0, 0, i))
    return pl.pallas_call(
        bwd_kernel,
        out_shape=(jax.ShapeDtypeStruct((TOK, WIDTH), BF),) * 3
        + (jax.ShapeDtypeStruct((2, SUMS, WIDTH), BF),),
        grid_spec=pltpu.PrefetchScalarGridSpec(
            num_scalar_prefetch=1,
            grid=(2,),
            in_specs=[pl.BlockSpec(memory_space=pltpu.VMEM)] * 4 + [prompt] + [pl.BlockSpec((4, TOK), lambda i, s: (0, 0))] * 4,
            out_specs=(rows, rows, rows, prompt),
            scratch_shapes=[
                pltpu.VMEM((wide, TOK), BF),
                pltpu.VMEM((wide, PAD), BF),
                pltpu.VMEM((wide, TOK), BF),
                pltpu.VMEM((TOK, wide), F32),
                pltpu.VMEM((TOK, wide), F32),
                pltpu.VMEM((PAD, wide), F32),
                pltpu.VMEM((PAD, wide), F32),
                pltpu.VMEM((PAD, wide), BF),
                pltpu.VMEM((PAD, wide), BF),
                pltpu.VMEM((8, TOK), F32),
            ],
        ),
        compiler_params=pltpu.CompilerParams(vmem_limit_bytes=36 << 20),
        cost_estimate=pl.CostEstimate(
            flops=16 * 5 * 2 * 896 * 256 * 256, transcendentals=16 * 896 * 256, bytes_accessed=10000000
        ),
        name="attend_back",
    )(scalars, q, k, v, g, prompts, *lses)


WCOLS = 640


def weight_kernel(bys, calls, s_ref, *refs):
    owns, others, g_ref, h_ref = refs[:calls], refs[calls : 2 * calls], refs[2 * calls], refs[2 * calls + 1]
    outs, picked = refs[2 * calls + 2 : -1], refs[-1]
    for n, by in enumerate(bys):
        quad = (s_ref[1] + by) & (SIDE - 1)
        for j in range(2 * calls):

            @pl.when(quad == s_ref[ORDER + j])
            def _():
                picked[n, 0] = owns[j // 2][j % 2]
                picked[n, 1] = others[j // 2][j % 2]

    for n, out_ref in enumerate(outs):
        for part in range(HALF // WCOLS):
            w = pl.ds(pl.multiple_of(s_ref[0] * HALF + part * WCOLS, 128), WCOLS)
            out = dot(picked[n, 0], g_ref[:, w]) + dot(picked[n, 1], h_ref[:, w])
            for sub in range(SIDE):
                for tile in range(WCOLS // 128):
                    out_ref[sub, part * (WCOLS // 128) + tile] = out[
                        sub * SUB : sub * SUB + SUB, tile * 128 : tile * 128 + 128
                    ].astype(out_ref.dtype)


def weight_quads(bys, scalars, owns, others, grad_rows, grad_other):
    count, calls = len(bys), len(owns)
    vmem = pl.BlockSpec(memory_space=pltpu.VMEM)
    outs = pl.pallas_call(
        functools.partial(weight_kernel, bys, calls),
        out_shape=[jax.ShapeDtypeStruct((SIDE, TILES, SUB, 128), BF if by else F32) for by in bys],
        in_specs=[pl.BlockSpec(memory_space=pltpu.SMEM)] + [vmem] * (2 * calls + 2),
        out_specs=[vmem] * count,
        scratch_shapes=[pltpu.VMEM((count, 2, QUAD, TOK), BF)],
        compiler_params=pltpu.CompilerParams(vmem_limit_bytes=16 << 20),
        cost_estimate=pl.CostEstimate(
            flops=count * 4 * QUAD * TOK * HALF, transcendentals=0, bytes_accessed=4200000
        ),
        name="weight_quads",
    )(scalars, *owns, *others, grad_rows, grad_other)
    return [out.reshape(SIDE, PIECE, 128) for out in outs]


def line_kernel(s_ref, own, r1, r2, r3, *outs):
    for by, out in enumerate(outs):
        n = (s_ref[2] + by) & (SIDE - 1)
        total = (own[n] + r2[n].astype(F32)) + (r1[n].astype(F32) + r3[n].astype(F32))
        out[...] = total.astype(out.dtype)


def sum_line(scalars, own, r1, r2, r3):
    vmem = pl.BlockSpec(memory_space=pltpu.VMEM)
    return pl.pallas_call(
        line_kernel,
        out_shape=[jax.ShapeDtypeStruct((PIECE, 128), kind) for kind in (F32, BF, BF, BF)],
        in_specs=[pl.BlockSpec(memory_space=pltpu.SMEM)] + [vmem] * 4,
        out_specs=[vmem] * 4,
        compiler_params=pltpu.CompilerParams(vmem_limit_bytes=8 << 20),
        cost_estimate=pl.CostEstimate(flops=2000000, transcendentals=0, bytes_accessed=5000000),
        name="sum_line",
    )(scalars, own, r1, r2, r3)


def order_kernel(s_ref, o_ref):
    segment, chip = s_ref[0], s_ref[1]
    x, y, z = chip & 3, (chip >> 2) & 3, chip >> 4
    p0 = (x + 2) & 3
    p1 = jnp.where(x == y, x + 1, y + 2) & 3
    p2 = (p0 + jnp.where(((p0 + 1) & 3) == p1, 2, 1)) & 3
    turn = jnp.where(segment == 0, x, y)
    sub = jnp.where(segment == 0, z, x)
    for n, value in enumerate((segment, turn, sub, x, y, z, p0, p1, p2, 6 - p0 - p1 - p2)):
        o_ref[n] = value


def order_scalars(where):
    smem = pl.BlockSpec(memory_space=pltpu.SMEM)
    return pl.pallas_call(
        order_kernel,
        out_shape=jax.ShapeDtypeStruct((ORDER + SIDE,), jnp.int32),
        in_specs=[smem],
        out_specs=smem,
        compiler_params=pltpu.CompilerParams(vmem_limit_bytes=1 << 20),
        cost_estimate=pl.CostEstimate(flops=6000000000, transcendentals=0, bytes_accessed=64),
        name="order",
    )(where)


def mid_kernel(own, r1, r2, r3, out):
    total = (own[...] + r2[...].astype(F32)) + (r1[...].astype(F32) + r3[...].astype(F32))
    out[...] = total.astype(BF)


def sum_mid(own, r1, r2, r3):
    return pl.pallas_call(
        mid_kernel,
        out_shape=jax.ShapeDtypeStruct((PIECE, 128), BF),
        compiler_params=pltpu.CompilerParams(vmem_limit_bytes=8 << 20),
        cost_estimate=pl.CostEstimate(flops=400000, transcendentals=0, bytes_accessed=1200000),
        name="sum_mid",
    )(own, r1, r2, r3)


def cross_kernel(own, r1, r2, r3, out):
    total = (own[...].astype(F32) + r2[...].astype(F32)) + (r1[...].astype(F32) + r3[...].astype(F32))
    out[:PIECE] = total.astype(BF)
    square = jnp.sum(total * total, 0, keepdims=True)
    terms = split_three(square)
    out[PIECE:] = jnp.concatenate(terms + (jnp.zeros((STAT - 3, 128), BF),), 0)


def sum_cross(own, r1, r2, r3):
    return pl.pallas_call(
        cross_kernel,
        out_shape=jax.ShapeDtypeStruct((PIECE + STAT, 128), BF),
        compiler_params=pltpu.CompilerParams(vmem_limit_bytes=8 << 20),
        cost_estimate=pl.CostEstimate(flops=600000, transcendentals=0, bytes_accessed=1200000),
        name="sum_cross",
    )(own, r1, r2, r3)


def split_three(x):
    high = x.astype(BF)
    rest = x - high.astype(F32)
    mid = rest.astype(BF)
    return high, mid, (rest - mid.astype(F32)).astype(BF)


def final_kernel(s_ref, *refs):
    pieces, later, out_hbm, dpk_hbm, dpv_hbm = refs[:8], refs[8], refs[9], refs[10], refs[11]
    outs, out_sem = refs[12:]
    hand = [
        pltpu.make_async_copy(later.at[n], to, out_sem.at[8 + n]) for n, to in enumerate((dpk_hbm, dpv_hbm))
    ]
    for move in hand:
        move.start()
    segment, x, y, z = s_ref[0], s_ref[3], s_ref[4], s_ref[5]
    total = jnp.zeros((1, 128), F32)
    for piece in pieces:
        for p in range(SIDE):
            total = total + jnp.sum(piece[p, PIECE : PIECE + STAT, :].astype(F32), 0, keepdims=True)
    mean = jnp.sum(total, 1, keepdims=True) * (1.0 / (WIDTH * D))
    scale = jnp.minimum(1.0, 1.0 / jnp.sqrt(mean + 1e-06))
    writes = []
    for n in range(8):
        k = n % 4
        half = segment if n < 4 else 1 - segment
        quad = (jnp.where(half == 0, x, y) + SIDE - k) % SIDE
        at = jnp.where(half == 0, z, x)
        for p in range(SIDE):
            rows = pl.ds(pl.multiple_of((at + SIDE - p) % SIDE * SUB, 16), SUB)
            for tile in range(TILES):
                outs[n, rows, tile * 128 : tile * 128 + 128] = (
                    pieces[n][p, tile * SUB : tile * SUB + SUB, :].astype(F32) * scale
                ).astype(BF)
        write = pltpu.make_async_copy(
            outs.at[n],
            out_hbm.at[
                pl.ds(pl.multiple_of(quad * QUAD, 64), QUAD), pl.ds(pl.multiple_of(half * HALF, 128), HALF)
            ],
            out_sem.at[n],
        )
        write.start()
        writes.append(write)
    for write in writes + hand:
        write.wait()


def finish(scalars, pieces, later):
    vmem, any_spec = pl.BlockSpec(memory_space=pltpu.VMEM), pl.BlockSpec(memory_space=pl.ANY)
    return pl.pallas_call(
        final_kernel,
        out_shape=(jax.ShapeDtypeStruct((WIDTH, D), BF),) + (jax.ShapeDtypeStruct((SUMS, WIDTH), BF),) * 2,
        in_specs=[pl.BlockSpec(memory_space=pltpu.SMEM)] + [vmem] * 8 + [any_spec],
        out_specs=(any_spec,) * 3,
        scratch_shapes=[
            pltpu.VMEM((8, QUAD, HALF), BF),
            pltpu.SemaphoreType.DMA((10,)),
        ],
        compiler_params=pltpu.CompilerParams(vmem_limit_bytes=16 << 20),
        cost_estimate=pl.CostEstimate(flops=7000000, transcendentals=0, bytes_accessed=14000000),
        name="clip",
    )(scalars, *pieces, later)


def hop(chip, axis, by):
    stride = {"x": 1, "y": SIDE, "z": SIDE * SIDE}[axis]
    at = (chip // stride) % SIDE
    return chip + (((at + by) % SIDE) - at) * stride


CHIPS = SIDE**3


def along(first, second, by):
    return [(c, hop(c, first, by)) for c in range(CHIPS)] + [
        (CHIPS + c, CHIPS + hop(c, second, by)) for c in range(CHIPS)
    ]


BOTH = ("seg", "dp")
SWAP = [(0, 1), (1, 0)]


def exchange(parts, first, second):
    received = []
    for by, part in zip((1, 2, 3), parts):
        received.append(lax.ppermute(part, BOTH, along(first, second, by)))
    return received


def program(query_rows, key_rows, value_rows, prompt_keys, prompt_values, out_grad, w_out):
    q, k, v, grad_rows = query_rows[0], key_rows[0], value_rows[0], out_grad[0]
    grad_other = lax.ppermute(grad_rows, "seg", SWAP)
    where = jnp.stack([lax.axis_index("seg"), lax.axis_index("dp")]).astype(jnp.int32)
    scalars, prompts = lax.optimization_barrier(
        (order_scalars(where), jnp.stack([prompt_keys[0], prompt_values[0]]))
    )
    prompts = lax.ppermute(prompts, "seg", [(0, 1)])

    attn, other, lses, sent = [], [], [], {}

    def forward(places, after=()):
        outs, stats = forward_quads(places, scalars, q, k, v, prompts, after)
        attn.append(outs)
        lses.extend(stats)
        other.append(lax.ppermute(outs, "seg", SWAP))

    def send(bys):
        parts = weight_quads(bys, scalars, attn, other, grad_rows, grad_other)
        for by, part in zip(bys, parts):
            sent[by] = lax.ppermute(part, BOTH, along("x", "y", by)) if by else part
        return parts

    forward((0, 1))
    forward((2, 3), send((2,)))
    send((1, 3))
    send((0,))
    head_low = jnp.einsum("td,hd->th", grad_rows, w_out, preferred_element_type=F32).astype(BF)
    sent, head_low = lax.optimization_barrier((sent, head_low))
    own, *rest = sum_line(scalars, sent[0], sent[1], sent[2], sent[3])
    own = sum_mid(own, *exchange(rest, "z", "x"))
    own = sum_cross(own, *exchange([own] * 3, "y", "z"))
    own = jnp.stack([own] + exchange([own] * 3, "z", "x"))

    own, head_low = lax.optimization_barrier((own, head_low))
    pieces = exchange([own] * 3, "x", "y")
    dq, dk, dv, dp = backward(scalars, q, k, v, head_low, prompts, lses)
    own, dp = lax.optimization_barrier((own, dp))
    later = lax.ppermute(dp, "seg", [(1, 0)])
    swapped = [lax.ppermute(own, "seg", SWAP)]
    for n in range(3):
        pieces[n], _ = lax.optimization_barrier((pieces[n], dp))
        swapped.append(lax.ppermute(pieces[n], "seg", SWAP))
    weight_grad, dpk, dpv = finish(scalars, [own] + pieces + swapped, later)
    return (dq[None], dk[None], dv[None], dpk[None], dpv[None], weight_grad)


def solution(mesh):
    rows = P("dp", "seg", None)
    return jax.shard_map(
        program,
        mesh=mesh,
        in_specs=(rows,) * 6 + (P(),),
        out_specs=(rows,) * 5 + (P(),),
        check_vma=False,
    )
```
